128 devices in a mesh: shot: 2 (over core), strip: 64 (over z, y, x).
Axes of the slice: x: 4, y: 4, z: 4, core: 2. Of those that a mesh axis runs over, the one named last changes fastest.
Arguments:
- source_now: float32 [2, 64, 2048, 256], P('shot', None, 'strip'), may hold values from -8 to 8
- source_prev: float32 [2, 64, 2048, 256], P('shot', None, 'strip'), may hold values from -8 to 8
- adjoint_now: float32 [2, 64, 2048, 256], P('shot', None, 'strip'), may hold values from -8 to 8
- adjoint_prev: float32 [2, 64, 2048, 256], P('shot', None, 'strip'), may hold values from -8 to 8
- courant: float32 [2048, 256], P('strip'), may hold values from 0.08 to 0.45
- probe_left: float32 [16, 2048, 256], P(None, 'strip'), may hold values from -6 to 6
- probe_right: float32 [16, 2048, 256], P(None, 'strip'), may hold values from -6 to 6
Outputs:
- left_factor: float32 [16, 2048, 256], P(None, 'strip')
- right_factor: float32 [16, 2048, 256], P(None, 'strip')
The draws below stay inside these ranges and needn't reach their ends.
All inputs are finite; a program needn't handle non-finite values.
Results may differ from the reference program's by a relative error of at most 0.0003.
Values sent between devices are 32-bit elements; how exact they have to be, the bound alone decides.
A program may use at most 64 MiB of HBM per device.

```python
import math
import jax
import jax.numpy as jnp
from jax import lax

NCOL = 256
SRC = 64
RANK = 16
STEPS = 8
GROUPS = 2
NROW = 2048


def wavefield(key, salt):
    base_key = jax.random.fold_in(key, salt)
    keys = jax.random.split(base_key, 2)
    shape = (GROUPS, SRC, NROW, NCOL)
    position = jnp.arange(NROW, dtype=jnp.float32) / max(NROW - 1, 1)
    cell_scale = 0.5 * jnp.exp(jax.random.uniform(keys[1], (1, 1, NROW, NCOL), minval=math.log(1.0 / 3.0), maxval=math.log(10.0 / 3.0)))
    noise = jax.random.normal(keys[0], shape)
    trend = (3.0 ** (position - 0.5))[:, None]
    values = noise * cell_scale * trend
    return jnp.clip(values, -8.0, 8.0).astype(jnp.float32)


def draw_source_now(key, part):
    return wavefield(key, 11)


def draw_source_prev(key, part):
    return wavefield(key, 23)


def draw_adjoint_now(key, part):
    return wavefield(key, 37)


def draw_adjoint_prev(key, part):
    return wavefield(key, 41)


def level_of(own_key, dims, pieces, smallest, largest):
    loudness = 1.0
    for dim, parts in pieces:
        steps = jax.random.uniform(jax.random.fold_in(jax.random.fold_in(own_key, 6), dim), (parts,), jnp.float32, smallest / len(pieces), largest / len(pieces))
        loudness = loudness * jnp.repeat(jnp.exp(steps), dims[dim] // parts).reshape((-1,) + (1,) * (len(dims) - 1 - dim))
    return loudness


def scatter_about(key, shape, deviation, limit, cuts=(), kind=jnp.bfloat16):
    gain = level_of(key, shape, cuts, -0.22, 0.18) if cuts else 1.0
    entries = jax.random.normal(key, shape, jnp.float32) * deviation * gain
    return jnp.minimum(jnp.maximum(entries, -limit), limit).astype(kind)


def setup_inputs(seed: int = 0) -> dict:
    streams_of = jax.random.split(jax.random.key(seed), 8)
    source_now = draw_source_now(jax.random.fold_in(streams_of[7], 71), 0)
    source_prev = draw_source_prev(jax.random.fold_in(streams_of[7], 71), 0)
    adjoint_now = draw_adjoint_now(jax.random.fold_in(streams_of[7], 71), 0)
    adjoint_prev = draw_adjoint_prev(jax.random.fold_in(streams_of[7], 71), 0)
    courant = jnp.clip(jnp.exp(math.log(0.45) - 1.7272209 * jax.random.uniform(streams_of[4], (NROW, NCOL), jnp.float32) ** level_of(streams_of[4], (NROW, NCOL), ((0, 64),), -0.2, 0.2)), 0.08, 0.45)
    probe_left = scatter_about(streams_of[5], (RANK, NROW, NCOL), 1.0, 6.0, ((1, 64),), jnp.float32)
    probe_right = scatter_about(streams_of[6], (RANK, NROW, NCOL), 1.0, 6.0, ((1, 64),), jnp.float32)
    return {"source_now": source_now, "source_prev": source_prev, "adjoint_now": adjoint_now, "adjoint_prev": adjoint_prev, "courant": courant, "probe_left": probe_left, "probe_right": probe_right}


def sideways(fields):
    zero_column = jnp.zeros_like(fields[..., :1])
    return jnp.concatenate([fields[..., 1:], zero_column], -1) + jnp.concatenate([zero_column, fields[..., :-1]], -1)

def leapfrog(field_now, field_prev, courant):
    zero_row = jnp.zeros_like(field_now[:, :1, :])
    above = jnp.concatenate([field_now[:, 1:, :], zero_row], 1)
    below = jnp.concatenate([zero_row, field_now[:, :-1, :]], 1)
    laplace = above + below + sideways(field_now) - 4.0 * field_now
    return 2.0 * field_now - field_prev + courant[None] * laplace

def orthonormal(sketch_sum):
    gram_value = jnp.dot(sketch_sum, sketch_sum.T, precision=lax.Precision.HIGHEST)
    lower_factor = jnp.linalg.cholesky(gram_value)
    solved = lax.linalg.triangular_solve(lower_factor, sketch_sum, left_side=True, lower=True)
    return (solved * math.sqrt(NROW * NCOL)).reshape(RANK, NROW, NCOL)

def reference(source_now, source_prev, adjoint_now, adjoint_prev, courant, probe_left, probe_right):
    flat_left = probe_left.reshape(RANK, -1)
    flat_right = probe_right.reshape(RANK, -1)

    def one_group(members):
        src_a, src_b, adj_a, adj_b = members
        field_now = jnp.concatenate([src_a, adj_a], 0)
        field_prev = jnp.concatenate([src_b, adj_b], 0)
        for step_index in range(STEPS):
            field_next = leapfrog(field_now, field_prev, courant)
            field_prev, field_now = (field_now, field_next)
        flat_source = field_now[:SRC].reshape(SRC, -1)
        flat_adjoint = field_now[SRC:].reshape(SRC, -1)
        left_probe = jnp.dot(flat_adjoint, flat_left.T, precision=lax.Precision.HIGHEST)
        right_probe = jnp.dot(flat_source, flat_right.T, precision=lax.Precision.HIGHEST)
        left_term = jnp.dot(left_probe.T, flat_source, precision=lax.Precision.HIGHEST)
        right_term = jnp.dot(right_probe.T, flat_adjoint, precision=lax.Precision.HIGHEST)
        return (left_term, right_term)
    left_terms, right_terms = lax.map(one_group, (source_now, source_prev, adjoint_now, adjoint_prev))
    left_sketch = lax.optimization_barrier(jnp.sum(left_terms, axis=0))
    right_sketch = lax.optimization_barrier(jnp.sum(right_terms, axis=0))
    return (orthonormal(left_sketch), orthonormal(right_sketch))
```

```python
import functools
import math

import jax
import jax.numpy as jnp
from jax import lax
from jax.experimental import pallas as pl
from jax.experimental.pallas import tpu as pltpu
from jax.sharding import PartitionSpec as P

STEPS = 8
SIDE = 4
MESH = pl.DeviceIdType.MESH
HIGHEST = lax.Precision.HIGHEST


def allreduce_kernel(x_ref, o_ref, part, recv, send_sem, recv_sem):
    me = lax.axis_index("strip")

    def peer(axis, distance):
        stride = SIDE**axis
        place = (me // stride) % SIDE
        return me + ((place + distance) % SIDE - place) * stride

    barrier = pltpu.get_barrier_semaphore()
    for axis in range(3):
        for distance in range(1, SIDE):
            pl.semaphore_signal(barrier, inc=1, device_id={"strip": peer(axis, distance)}, device_id_type=MESH)
    pl.semaphore_wait(barrier, 3 * (SIDE - 1))
    for axis in range(3):
        source = x_ref if axis == 0 else part.at[axis - 1]
        copies = []
        for distance in range(1, SIDE):
            copy = pltpu.make_async_remote_copy(
                src_ref=source,
                dst_ref=recv.at[axis, distance - 1],
                send_sem=send_sem.at[axis, distance - 1],
                recv_sem=recv_sem.at[axis, distance - 1],
                device_id={"strip": peer(axis, distance)},
                device_id_type=MESH,
            )
            copy.start()
            copies.append(copy)
        total = source[...]
        for distance in range(1, SIDE):
            copies[distance - 1].wait_recv()
            total = total + recv[axis, distance - 1]
        if axis == 2:
            o_ref[...] = total
        else:
            part[axis] = total
        for copy in copies:
            copy.wait_send()


def allreduce(x, collective_id):
    return pl.pallas_call(
        allreduce_kernel,
        out_shape=jax.ShapeDtypeStruct(x.shape, jnp.float32),
        in_specs=[pl.BlockSpec(memory_space=pltpu.VMEM)],
        out_specs=pl.BlockSpec(memory_space=pltpu.VMEM),
        scratch_shapes=[
            pltpu.VMEM((2,) + x.shape, jnp.float32),
            pltpu.VMEM((3, SIDE - 1) + x.shape, jnp.float32),
            pltpu.SemaphoreType.DMA((3, SIDE - 1)),
            pltpu.SemaphoreType.DMA((3, SIDE - 1)),
        ],
        compiler_params=pltpu.CompilerParams(collective_id=collective_id, has_side_effects=True),
        name="strip_sum%d" % collective_id,
    )(x)


def extended(cells, dim, width):
    count = lax.axis_size("strip")
    head = lax.slice_in_dim(cells, 0, width, axis=dim)
    tail = lax.slice_in_dim(cells, cells.shape[dim] - width, cells.shape[dim], axis=dim)
    return jnp.concatenate(
        [
            lax.ppermute(tail, "strip", [(i, i + 1) for i in range(count - 1)]),
            cells,
            lax.ppermute(head, "strip", [(i + 1, i) for i in range(count - 1)]),
        ],
        axis=dim,
    )


def neighbours(f):
    col = jnp.zeros_like(f[..., :1])
    row = jnp.zeros_like(f[:, :1])
    side = jnp.concatenate([f[..., 1:], col], -1) + jnp.concatenate([col, f[..., :-1]], -1)
    vert = jnp.concatenate([f[:, 1:], row], 1) + jnp.concatenate([row, f[:, :-1]], 1)
    return side + vert - 4.0 * f


def dot(a, b, dims):
    return lax.dot_general(a, b, (dims, ((), ())), precision=HIGHEST)


def shards(source_now, source_prev, adjoint_now, adjoint_prev, courant, probe_left, probe_right):
    src_now, src_prev, adj_now, adj_prev = (a[0] for a in (source_now, source_prev, adjoint_now, adjoint_prev))
    rank = probe_left.shape[0]
    rows, cols = courant.shape
    speed = extended(courant, 0, STEPS)[None]
    now = extended(jnp.concatenate([probe_left, probe_right], 0), 1, STEPS)
    prev = jnp.zeros_like(now)
    for _ in range(STEPS):
        now, prev = 2.0 * now + neighbours(speed * now) - prev, now
    now, prev = now[:, STEPS:-STEPS], prev[:, STEPS:-STEPS]
    cells = ((1, 2), (1, 2))
    left = dot(now[:rank], adj_now, cells) - dot(prev[:rank], adj_prev, cells)
    right = dot(now[rank:], src_now, cells) - dot(prev[rank:], src_prev, cells)
    weight = allreduce(jnp.concatenate([left, right], 1), 0)
    left, right = weight[:, : left.shape[1]], weight[:, left.shape[1] :]
    wave = ((1,), (0,))
    now = jnp.concatenate([dot(left, src_now, wave), dot(right, adj_now, wave)], 0)
    prev = jnp.concatenate([dot(left, src_prev, wave), dot(right, adj_prev, wave)], 0)
    now, prev = lax.psum((now, prev), "shot")
    now, prev = extended(now, 1, STEPS), extended(prev, 1, STEPS)
    for _ in range(STEPS):
        now, prev = 2.0 * now + speed * neighbours(now) - prev, now
    sketch = now[:, STEPS:-STEPS]
    left, right = sketch[:rank], sketch[rank:]
    grams = jnp.concatenate([dot(left, left, cells), dot(right, right, cells)], 1)
    grams = allreduce(jnp.pad(grams, ((0, 0), (0, 128 - 2 * rank))), 1)
    scale = math.sqrt(rows * lax.axis_size("strip") * cols)

    def orthonormal(fields, gram):
        lower = jnp.linalg.cholesky(gram)
        solved = lax.linalg.triangular_solve(lower, fields.reshape(rank, -1), left_side=True, lower=True)
        return (solved * scale).reshape(fields.shape)

    return orthonormal(left, grams[:, :rank]), orthonormal(right, grams[:, rank : 2 * rank])


def solution(mesh):
    return jax.shard_map(
        shards,
        mesh=mesh,
        in_specs=(P("shot", None, "strip", None),) * 4 + (P("strip", None),) + (P(None, "strip", None),) * 2,
        out_specs=(P(None, "strip", None), P(None, "strip", None)),
        check_vma=False,
    )
```

```python
import functools
import math

import jax
import jax.numpy as jnp
from jax import lax
from jax.experimental import pallas as pl
from jax.experimental.pallas import tpu as pltpu
from jax.sharding import PartitionSpec as P

STEPS = 8
WAVES = 64
RANK = 16
ROWS = 32
COLS = 256
HALF = 128
TALL = ROWS + 2 * STEPS
SIDE = 4
PLANE = SIDE * SIDE
MESH = pl.DeviceIdType.MESH
F32 = jnp.float32
BF16 = jnp.bfloat16


def split(x):
    high = x.astype(BF16)
    low = (x - high.astype(F32)).astype(BF16)
    return high, low


def stacked(x):
    return jnp.concatenate(split(x), 0)


def dot_rows(a, b):
    return lax.dot_general(a, b, (((1,), (1,)), ((), ())), preferred_element_type=F32)


def dot(a, b):
    return lax.dot_general(a, b, (((1,), (0,)), ((), ())), preferred_element_type=F32)


def sideways(x):
    lane = lax.broadcasted_iota(jnp.int32, (RANK, HALF), 1)
    first, second = x[:, :HALF], x[:, HALF:]
    ahead0, ahead1 = pltpu.roll(first, 1, 1), pltpu.roll(second, 1, 1)
    back0, back1 = pltpu.roll(first, HALF - 1, 1), pltpu.roll(second, HALF - 1, 1)
    start, end = lane == 0, lane == HALF - 1
    out0 = jnp.where(start, 0.0, ahead0) + jnp.where(end, back1, back0)
    out1 = jnp.where(start, ahead0, ahead1) + jnp.where(end, 0.0, back1)
    return jnp.concatenate([out0, out1], 1)


def twice(x):
    return jnp.concatenate([x, x], 0)


def sweep(buf, speed, middle, level, low, pairs, transposed):
    now = buf.at[lax.rem(level + 1, 2)]
    new = buf.at[lax.rem(level, 2)]

    def term(r):
        if transposed:
            return twice(speed[r]) * now[r]
        return now[r]

    def put(r, above, centre, below):
        spread = above + below + sideways(centre)
        if not transposed:
            spread = twice(speed[r]) * spread
        new[r] = twice(middle[r]) * now[r] - new[r] + spread

    def body(i, carry):
        above, centre = carry
        r = low + 2 * i
        below = term(r + 1)
        put(r, above, centre, below)
        beyond = term(r + 2)
        put(r + 1, centre, below, beyond)
        return below, beyond

    lax.fori_loop(0, pairs, body, (term(low - 1), term(low)))


def inner_sweeps(buf, speed, middle, transposed):
    def body(level, carry):
        sweep(buf, speed, middle, level, STEPS + level, ROWS // 2 - level, transposed)
        return carry

    lax.fori_loop(1, STEPS + 1, body, 0)


def edge_sweeps(buf, speed, middle, transposed):
    def body(level, carry):
        sweep(buf, speed, middle, level, level, STEPS // 2, transposed)
        sweep(buf, speed, middle, level, STEPS + ROWS - level, STEPS // 2, transposed)
        return carry

    lax.fori_loop(1, STEPS + 1, body, 0)


def lower_inverse(gram):
    row = lax.broadcasted_iota(jnp.int32, (RANK, HALF), 0)
    lane = lax.broadcasted_iota(jnp.int32, (RANK, HALF), 1)
    work = jnp.where(lane < RANK, gram, jnp.where(lane == row + RANK, 1.0, 0.0))
    for k in range(RANK):
        pivot = work[k : k + 1, k : k + 1]
        root = 1.0 / jnp.sqrt(pivot)
        line = work[k : k + 1, :] * root
        column = jnp.where(row[:, :1] > k, work[:, k : k + 1] * root, 0.0)
        work = jnp.where(row == k, line, work - column * line)
    return work


def main_kernel(
    src_now, src_prev, adj_now, adj_prev, courant, left3, right3, left2, right2,
    s_out, inv_out,
    waves, slabs, probes, probe_edges, speed_own, speed_edges, speed, middle,
    steps_p, weights, plane_send, plane_recv, column_send, column_recv, other_gram,
    fields, partial, arrived,
    load_sem, edge_send, edge_recv, sum_send, sum_recv, core_send, core_recv, halo_send, halo_recv, out_sem,
):
    own = lax.axis_index("shot")
    me = lax.axis_index("strip")
    count = lax.axis_size("strip")
    x, y, z = me % SIDE, (me // SIDE) % SIDE, me // PLANE
    after, before = (me + 1) % count, (me + count - 1) % count
    lane = lax.broadcasted_iota(jnp.int32, (RANK, HALF), 1)

    def plane_peer(d):
        return z * PLANE + ((y + d // SIDE) % SIDE) * SIDE + (x + d % SIDE) % SIDE

    def column_peer(d):
        return ((z + d) % SIDE) * PLANE + y * SIDE + x

    def remote(src, dst, send, recv, device):
        return pltpu.make_async_remote_copy(
            src_ref=src, dst_ref=dst, send_sem=send, recv_sem=recv, device_id=device, device_id_type=MESH
        )

    barrier = pltpu.get_barrier_semaphore()
    strips = [plane_peer(d) for d in range(1, PLANE)] + [column_peer(d) for d in range(1, SIDE)] + [after, before]
    for peer in strips:
        pl.semaphore_signal(barrier, inc=1, device_id={"strip": peer}, device_id_type=MESH)
    pl.semaphore_signal(barrier, inc=1, device_id={"shot": 1 - own}, device_id_type=MESH)

    halves = [pl.ds(0, HALF), pl.ds(HALF, HALF)]
    loads = [pltpu.make_async_copy(courant, speed_own, load_sem.at[0])]
    for k, probe in enumerate((left2, right2)):
        for h in range(2):
            loads.append(pltpu.make_async_copy(probe.at[:, halves[h]], probes.at[k, h], load_sem.at[1 + 2 * k + h]))
    for a, wave in enumerate((src_now, src_prev, adj_now, adj_prev)):
        for h in range(2):
            loads.append(pltpu.make_async_copy(wave.at[:, halves[h]], waves.at[a, h], load_sem.at[5 + 2 * a + h]))
    for load in loads:
        load.start()

    pl.semaphore_wait(barrier, len(strips) + 1)

    edges = []
    for side, (target, first) in enumerate(((after, ROWS - STEPS), (before, 0))):
        edges.append(
            remote(courant.at[pl.ds(first, STEPS)], speed_edges.at[side],
                   edge_send.at[side, 0], edge_recv.at[side, 0], {"strip": target})
        )
    for k, probe in enumerate((left3, right3)):
        for side, (target, first) in enumerate(((after, ROWS - STEPS), (before, 0))):
            for h in range(2):
                at = 1 + 2 * k + h
                edges.append(
                    remote(probe.at[:, pl.ds(first, STEPS), halves[h]], probe_edges.at[side, k, h],
                           edge_send.at[side, at], edge_recv.at[side, at], {"strip": target})
                )
    for copy in edges:
        copy.start()

    def put_speed(values, row0):
        for r in range(STEPS):
            value = jnp.broadcast_to(values[r : r + 1, :], (8, COLS))
            speed[row0 + r] = value
            middle[row0 + r] = 2.0 - 4.0 * value

    loads[0].wait()
    for block in range(ROWS // STEPS):
        put_speed(speed_own[pl.ds(block * STEPS, STEPS), :], STEPS + block * STEPS)
    for load in loads[1:5]:
        load.wait()

    def put_probe(r, carry):
        for k in range(2):
            steps_p[k, 0, STEPS + r] = jnp.concatenate(
                [probes[k, h, pl.ds(r, RANK, stride=ROWS), :] for h in range(2)], 1
            )
        return carry

    lax.fori_loop(0, ROWS, put_probe, 0)

    def put_zero(r, carry):
        for k in range(2):
            steps_p[k, 1, r] = jnp.zeros((RANK, COLS), F32)
        return carry

    lax.fori_loop(0, TALL, put_zero, 0)

    for k in range(2):
        inner_sweeps(steps_p.at[k], speed, middle, True)

    for a in range(4):
        loads[5 + 2 * a].wait()
        loads[6 + 2 * a].wait()

        def put_slab(r, carry):
            value = jnp.concatenate([waves[a, h, pl.ds(r, WAVES, stride=ROWS), :] for h in range(2)], 1)
            slabs[a, r] = stacked(value)
            return carry

        lax.fori_loop(0, ROWS, put_slab, 0)

    def products(r, totals):
        out = []
        for k in range(2):
            total = totals[k]
            a = 2 - 2 * k
            total = total + dot_rows(stacked(steps_p[k, 0, STEPS + r]), slabs[a, r])
            total = total - dot_rows(stacked(steps_p[k, 1, STEPS + r]), slabs[a + 1, r])
            out.append(total)
        return tuple(out)

    zero = jnp.zeros((2 * RANK, HALF), F32)
    totals = lax.fori_loop(STEPS, ROWS - STEPS, products, (zero, zero))

    for copy in edges:
        copy.wait_recv()
    inside = (me > 0, me < count - 1)
    for side, row0 in enumerate((0, STEPS + ROWS)):
        put_speed(jnp.where(inside[side], speed_edges[side], 0.0), row0)
        for k in range(2):
            for r in range(STEPS):
                steps_p[k, 0, row0 + r] = jnp.concatenate(
                    [probe_edges.at[side, k, h].reshape(RANK * STEPS, HALF)[pl.ds(r, RANK, stride=STEPS), :] for h in range(2)], 1
                )
    for k in range(2):
        edge_sweeps(steps_p.at[k], speed, middle, True)
    totals = lax.fori_loop(0, STEPS, products, totals)
    totals = lax.fori_loop(ROWS - STEPS, ROWS, products, totals)

    def strip_sum(value, i):
        plane_send[i] = value
        copies = [
            remote(plane_send.at[i], plane_recv.at[i, d - 1], sum_send.at[i, d - 1], sum_recv.at[i, d - 1],
                   {"strip": plane_peer(d)})
            for d in range(1, PLANE)
        ]
        for copy in copies:
            copy.start()
        for d, copy in enumerate(copies):
            copy.wait_recv()
            value = value + plane_recv[i, d]
        column_send[i] = value
        more = [
            remote(column_send.at[i], column_recv.at[i, d - 1], sum_send.at[i, PLANE + d - 2],
                   sum_recv.at[i, PLANE + d - 2], {"strip": column_peer(d)})
            for d in range(1, SIDE)
        ]
        for copy in more:
            copy.start()
        for d, copy in enumerate(more):
            copy.wait_recv()
            value = value + column_recv[i, d]
        for copy in copies + more:
            copy.wait_send()
        return value

    folded = []
    for k in range(2):
        both = totals[k][:RANK] + totals[k][RANK:]
        folded.append(both + pltpu.roll(both, WAVES, 1))
    weight = strip_sum(jnp.where(lane < WAVES, folded[0], folded[1]), 0)
    turned = pltpu.roll(weight, WAVES, 1)
    weights[0] = stacked(jnp.where(lane < WAVES, weight, turned))
    weights[1] = stacked(jnp.where(lane < WAVES, turned, weight))

    def combine(side, level, r):
        both = dot(weights[side], slabs[2 * side + level, r])
        return both[:RANK] + both[RANK:]

    away = 1 - own

    def for_other(r, carry):
        for level in range(2):
            partial[level, r] = combine(away, level, r)
        return carry

    def for_own(r, carry):
        for level in range(2):
            fields[level, STEPS + r] = combine(own, level, r)
        return carry

    def add_arrived(r, carry):
        for level in range(2):
            fields[level, STEPS + r] = fields[level, STEPS + r] + arrived[level, r]
        return carry

    spans = ((0, STEPS), (ROWS - STEPS, ROWS), (STEPS, ROWS - STEPS))

    def core_copies(index):
        lo, hi = spans[index]
        return [
            remote(partial.at[level, pl.ds(lo, hi - lo)], arrived.at[level, pl.ds(lo, hi - lo)],
                   core_send.at[2 * index + level], core_recv.at[2 * index + level], {"shot": away})
            for level in range(2)
        ]

    crossing = []
    for index in range(2):
        lax.fori_loop(*spans[index], for_other, 0)
        copies = core_copies(index)
        for copy in copies:
            copy.start()
        crossing.append(copies)
    halos = []
    for index in range(2):
        lax.fori_loop(*spans[index], for_own, 0)
    for index in range(2):
        for copy in crossing[index]:
            copy.wait_recv()
        lax.fori_loop(*spans[index], add_arrived, 0)
        target, landing = ((before, STEPS + ROWS), (after, 0))[index]
        start = STEPS + spans[index][0]
        skip = index
        for level in range(2):
            at = level * skip
            copy = remote(
                fields.at[level, pl.ds(start + at, STEPS - level)],
                fields.at[level, pl.ds(landing + at, STEPS - level)],
                halo_send.at[index, level], halo_recv.at[index, level], {"strip": target},
            )
            copy.start()
            halos.append(copy)
    lax.fori_loop(*spans[2], for_other, 0)
    crossing.append(core_copies(2))
    for copy in crossing[2]:
        copy.start()
    lax.fori_loop(*spans[2], for_own, 0)
    for copy in crossing[2]:
        copy.wait_recv()
    lax.fori_loop(*spans[2], add_arrived, 0)
    for copy in halos:
        copy.wait_send()
    inner_sweeps(fields, speed, middle, False)
    for copy in halos:
        copy.wait_recv()

    for side, row0 in enumerate((0, STEPS + ROWS)):
        @pl.when(jnp.logical_not(inside[side]))
        def _():
            for level in range(2):
                for r in range(STEPS):
                    fields[level, row0 + r] = jnp.zeros((RANK, COLS), F32)

    edge_sweeps(fields, speed, middle, False)

    results = [
        pltpu.make_async_copy(fields.at[0, pl.ds(STEPS, ROWS)], s_out.at[own], out_sem.at[0]),
        remote(fields.at[0, pl.ds(STEPS, ROWS)], s_out.at[own], core_send.at[6], core_recv.at[6], {"shot": away}),
    ]
    for copy in results:
        copy.start()

    def gram_rows(i, total):
        value = jnp.concatenate([stacked(fields[0, STEPS + 4 * i + j]) for j in range(4)], 1)
        return total + dot_rows(value, value)

    gram = lax.fori_loop(0, ROWS // 4, gram_rows, jnp.zeros((2 * RANK, 2 * RANK), F32))
    gram = gram[:RANK] + gram[RANK:]
    gram = gram[:, :RANK] + gram[:, RANK:]
    gram = strip_sum(jnp.concatenate([gram, jnp.zeros((RANK, HALF - RANK), F32)], 1), 1)
    plane_send[2] = gram
    swap = remote(plane_send.at[2], other_gram, core_send.at[7], core_recv.at[7], {"shot": away})
    swap.start()
    swap.wait()
    theirs = other_gram[...]
    flag = (own + jnp.zeros((RANK, HALF), jnp.int32)) == 0
    inv_out[0] = lower_inverse(jnp.where(flag, gram, theirs))
    inv_out[1] = lower_inverse(jnp.where(flag, theirs, gram))

    for copy in results:
        copy.wait()
    for copy in edges:
        copy.wait_send()
    for copies in crossing:
        for copy in copies:
            copy.wait_send()


def final_kernel(scale, s_ref, inv_ref, left_out, right_out, blocks, sem):
    copies = []
    for side, out in enumerate((left_out, right_out)):
        inverse = inv_ref[side] * scale
        left = inverse[:, RANK : 2 * RANK]
        high, low = split(left)
        lhs = jnp.concatenate([jnp.concatenate([high, high], 1), jnp.concatenate([low, low], 1)], 0)

        def body(r, carry):
            both = dot(lhs, stacked(s_ref[side, r]))
            value = both[:RANK] + both[RANK:]
            for h in range(2):
                blocks[side, h, pl.ds(r, RANK, stride=ROWS), :] = value[:, h * HALF : (h + 1) * HALF]
            return carry

        lax.fori_loop(0, ROWS, body, 0, unroll=4)
        for h in range(2):
            copy = pltpu.make_async_copy(blocks.at[side, h], out.at[:, pl.ds(h * HALF, HALF)], sem.at[side, h])
            copy.start()
            copies.append(copy)
    for copy in copies:
        copy.wait()


def shards(source_now, source_prev, adjoint_now, adjoint_prev, courant, probe_left, probe_right):
    waves = [a.reshape(WAVES * ROWS, COLS) for a in (source_now, source_prev, adjoint_now, adjoint_prev)]
    any_spec = pl.BlockSpec(memory_space=pl.ANY)
    vmem_spec = pl.BlockSpec(memory_space=pltpu.VMEM)
    dma = pltpu.SemaphoreType.DMA
    sketch, inverse = pl.pallas_call(
        main_kernel,
        out_shape=(
            jax.ShapeDtypeStruct((2, ROWS, RANK, COLS), F32),
            jax.ShapeDtypeStruct((2, RANK, HALF), F32),
        ),
        in_specs=[any_spec] * 9,
        out_specs=(any_spec, vmem_spec),
        scratch_shapes=[
            pltpu.VMEM((4, 2, WAVES * ROWS, HALF), F32),
            pltpu.VMEM((4, ROWS, 2 * WAVES, COLS), BF16),
            pltpu.VMEM((2, 2, RANK * ROWS, HALF), F32),
            pltpu.VMEM((2, 2, 2, RANK, STEPS, HALF), F32),
            pltpu.VMEM((ROWS, COLS), F32),
            pltpu.VMEM((2, STEPS, COLS), F32),
            pltpu.VMEM((TALL, 8, COLS), F32),
            pltpu.VMEM((TALL, 8, COLS), F32),
            pltpu.VMEM((2, 2, TALL, RANK, COLS), F32),
            pltpu.VMEM((2, 2 * RANK, HALF), BF16),
            pltpu.VMEM((3, RANK, HALF), F32),
            pltpu.VMEM((2, PLANE - 1, RANK, HALF), F32),
            pltpu.VMEM((2, RANK, HALF), F32),
            pltpu.VMEM((2, SIDE - 1, RANK, HALF), F32),
            pltpu.VMEM((RANK, HALF), F32),
            pltpu.VMEM((2, TALL, RANK, COLS), F32),
            pltpu.VMEM((2, ROWS, RANK, COLS), F32),
            pltpu.VMEM((2, ROWS, RANK, COLS), F32),
            dma((13,)),
            dma((2, 5)),
            dma((2, 5)),
            dma((2, PLANE + SIDE - 2)),
            dma((2, PLANE + SIDE - 2)),
            dma((8,)),
            dma((8,)),
            dma((2, 2)),
            dma((2, 2)),
            dma((1,)),
        ],
        compiler_params=pltpu.CompilerParams(
            collective_id=0, has_side_effects=True, vmem_limit_bytes=56 * 1024 * 1024
        ),
        name="sketch",
    )(*waves, courant, probe_left, probe_right, probe_left.reshape(RANK * ROWS, COLS), probe_right.reshape(RANK * ROWS, COLS))
    scale = math.sqrt(ROWS * lax.axis_size("strip") * COLS)
    outs = pl.pallas_call(
        functools.partial(final_kernel, scale),
        out_shape=(jax.ShapeDtypeStruct((RANK * ROWS, COLS), F32),) * 2,
        in_specs=[vmem_spec] * 2,
        out_specs=(any_spec, any_spec),
        scratch_shapes=[pltpu.VMEM((2, 2, RANK * ROWS, HALF), F32), dma((2, 2))],
        name="factors",
    )(sketch, inverse)
    return tuple(out.reshape(RANK, ROWS, COLS) for out in outs)


def solution(mesh):
    return jax.shard_map(
        shards,
        mesh=mesh,
        in_specs=(P("shot", None, "strip", None),) * 4 + (P("strip", None),) + (P(None, "strip", None),) * 2,
        out_specs=(P(None, "strip", None), P(None, "strip", None)),
        check_vma=False,
    )
```

```python
import functools
import math

import jax
import jax.numpy as jnp
from jax import lax
from jax.experimental import pallas as pl
from jax.experimental.pallas import tpu as pltpu
from jax.sharding import PartitionSpec as P

STEPS = 8
WAVES = 64
RANK = 16
ROWS = 32
COLS = 256
HALF = 128
TALL = ROWS + 2 * STEPS
SIDE = 4
PLANE = SIDE * SIDE
MESH = pl.DeviceIdType.MESH
F32 = jnp.float32
BF16 = jnp.bfloat16


def split(x):
    high = x.astype(BF16)
    low = (x - high.astype(F32)).astype(BF16)
    return high, low


def stacked(x):
    return jnp.concatenate(split(x), 0)


def dot_rows(a, b):
    return lax.dot_general(a, b, (((1,), (1,)), ((), ())), preferred_element_type=F32)


def dot(a, b):
    return lax.dot_general(a, b, (((1,), (0,)), ((), ())), preferred_element_type=F32)


def spread_of(cells, beside):
    count = cells.shape[0]
    both = dot(jnp.concatenate(split(cells.reshape(count * RANK, COLS)), 0), beside[...])
    return (both[: count * RANK] + both[count * RANK :]).reshape(count, 2, 8, COLS)


def load_rows(ref, low, count):
    return ref[pl.ds(low, count)].reshape(count, 2, 8, COLS)


def advance(buf, speed, middle, beside, level, starts, count, transposed):
    now = buf.at[lax.rem(level + 1, 2)]
    new = buf.at[lax.rem(level, 2)]
    pieces = []
    for low in starts:
        cells = load_rows(now, low - 1, count + 2)
        if transposed:
            cells = cells * speed[pl.ds(low - 1, count + 2)][:, None]
        pieces.append(cells)
    inner = [cells[1:-1] for cells in pieces]
    side = spread_of(inner[0] if len(inner) == 1 else jnp.concatenate(inner, 0), beside)
    for k, low in enumerate(starts):
        total = pieces[k][:-2] + pieces[k][2:] + side[k * count : (k + 1) * count]
        if not transposed:
            total = total * speed[pl.ds(low, count)][:, None]
        centre = load_rows(now, low, count) if transposed else inner[k]
        value = middle[pl.ds(low, count)][:, None] * centre - load_rows(new, low, count) + total
        new[pl.ds(low, count)] = value.reshape(count, RANK, COLS)


def inner_sweeps(buf, speed, middle, beside, transposed):
    for level in range(1, STEPS + 1):
        advance(buf, speed, middle, beside, level, (STEPS + level,), ROWS - 2 * level, transposed)


def edge_sweeps(buf, speed, middle, beside, transposed):
    def body(level, carry):
        advance(buf, speed, middle, beside, level, (level, STEPS + ROWS - level), STEPS, transposed)
        return carry

    lax.fori_loop(1, STEPS + 1, body, 0)


def lower_inverse(gram):
    row = lax.broadcasted_iota(jnp.int32, (RANK, HALF), 0)
    lane = lax.broadcasted_iota(jnp.int32, (RANK, HALF), 1)
    work = jnp.where(lane < RANK, gram, jnp.where(lane == row + RANK, 1.0, 0.0))
    for k in range(RANK):
        pivot = work[k : k + 1, k : k + 1]
        root = 1.0 / jnp.sqrt(pivot)
        line = work[k : k + 1, :] * root
        column = jnp.where(row[:, :1] > k, work[:, k : k + 1] * root, 0.0)
        work = jnp.where(row == k, line, work - column * line)
    return work


def main_kernel(
    src_now, src_prev, adj_now, adj_prev, courant, probe_left, probe_right,
    s_out, inv_out,
    waves, slabs, probes, probe_edges, speed_own, speed_edges, speed, middle, beside,
    steps_p, steps_other, weights, plane_send, plane_recv, column_send, column_recv, other_gram,
    fields, leaving, partial, arrived,
    load_sem, edge_send, edge_recv, sum_send, sum_recv, core_send, core_recv, halo_send, halo_recv,
    step_send, step_recv, out_sem,
):
    own = lax.axis_index("shot")
    away = 1 - own
    me = lax.axis_index("strip")
    count = lax.axis_size("strip")
    x, y, z = me % SIDE, (me // SIDE) % SIDE, me // PLANE
    after, before = (me + 1) % count, (me + count - 1) % count
    lane = lax.broadcasted_iota(jnp.int32, (RANK, HALF), 1)
    blocks = ROWS // STEPS
    targets = ((after, ROWS - STEPS), (before, 0))
    halves = [pl.ds(0, HALF), pl.ds(HALF, HALF)]

    def plane_peer(d):
        return z * PLANE + ((y + d // SIDE) % SIDE) * SIDE + (x + d % SIDE) % SIDE

    def column_peer(d):
        return ((z + d) % SIDE) * PLANE + y * SIDE + x

    def remote(src, dst, send, recv, device):
        return pltpu.make_async_remote_copy(
            src_ref=src, dst_ref=dst, send_sem=send, recv_sem=recv, device_id=device, device_id_type=MESH
        )

    barrier = pltpu.get_barrier_semaphore()
    strips = [plane_peer(d) for d in range(1, PLANE)] + [column_peer(d) for d in range(1, SIDE)] + [after, before]
    for peer in strips:
        pl.semaphore_signal(barrier, inc=1, device_id={"strip": peer}, device_id_type=MESH)
    pl.semaphore_signal(barrier, inc=1, device_id={"shot": away}, device_id_type=MESH)

    def probe_loads(probe):
        return [
            pltpu.make_async_copy(probe.at[:, pl.ds(b * STEPS, STEPS), halves[h]], probes.at[b, h], load_sem.at[1 + 2 * b + h])
            for b in range(blocks)
            for h in range(2)
        ]

    def probe_sends(probe):
        return [
            remote(probe.at[:, pl.ds(first, STEPS), halves[h]], probe_edges.at[side, h],
                   edge_send.at[side, 1 + h], edge_recv.at[side, 1 + h], {"strip": target})
            for side, (target, first) in enumerate(targets)
            for h in range(2)
        ]

    load_speed = pltpu.make_async_copy(courant, speed_own, load_sem.at[0])
    load_speed.start()
    for core, probe in enumerate((probe_left, probe_right)):
        @pl.when(own == core)
        def _():
            for load in probe_loads(probe):
                load.start()
    base = 1 + 2 * blocks
    loads = [
        [
            pltpu.make_async_copy(
                wave.at[:, pl.ds(b * STEPS, STEPS), halves[h]], waves.at[a, b, h],
                load_sem.at[base + (a * blocks + b) * 2 + h],
            )
            for b in range(blocks)
            for h in range(2)
        ]
        for a, wave in enumerate((src_now, src_prev, adj_now, adj_prev))
    ]
    for group in loads:
        for load in group:
            load.start()

    near = lax.broadcasted_iota(jnp.int32, (COLS, COLS), 0) - lax.broadcasted_iota(jnp.int32, (COLS, COLS), 1)
    beside[...] = jnp.where(jnp.abs(near) == 1, 1.0, 0.0).astype(BF16)

    def put_speed(values, row0):
        for r in range(STEPS):
            value = jnp.broadcast_to(values[r : r + 1, :], (8, COLS))
            speed[row0 + r] = value
            middle[row0 + r] = 2.0 - 4.0 * value

    load_speed.wait()
    for block in range(blocks):
        put_speed(speed_own[pl.ds(block * STEPS, STEPS), :], STEPS + block * STEPS)
    for load in probe_loads(probe_left):
        load.wait()

    def rows_of(tiles, b, r):
        return jnp.concatenate([
            tiles.at[b, h].reshape(RANK * STEPS, HALF)[pl.ds(r, RANK, stride=STEPS), :] for h in range(2)
        ], 1)

    for b in range(blocks):
        for r in range(STEPS):
            steps_p[0, STEPS + b * STEPS + r] = rows_of(probes, b, r)

    def put_zero(r, carry):
        steps_p[1, r] = jnp.zeros((RANK, COLS), F32)
        return carry

    lax.fori_loop(0, TALL, put_zero, 0)

    pl.semaphore_wait(barrier, len(strips) + 1)

    speed_sends = [
        remote(courant.at[pl.ds(first, STEPS)], speed_edges.at[side],
               edge_send.at[side, 0], edge_recv.at[side, 0], {"strip": target})
        for side, (target, first) in enumerate(targets)
    ]
    for copy in speed_sends:
        copy.start()
    for core, probe in enumerate((probe_left, probe_right)):
        @pl.when(own == core)
        def _():
            for copy in probe_sends(probe):
                copy.start()
    edges = speed_sends + probe_sends(probe_left)

    inner_sweeps(steps_p, speed, middle, beside, True)

    spans = ((0, STEPS), (ROWS - STEPS, ROWS), (STEPS, ROWS - STEPS))

    def hand_over(index):
        lo, hi = spans[index]
        copies = [
            remote(steps_p.at[level, pl.ds(STEPS + lo, hi - lo)], steps_other.at[level, pl.ds(lo, hi - lo)],
                   step_send.at[index, level], step_recv.at[index, level], {"shot": away})
            for level in range(2)
        ]
        for copy in copies:
            copy.start()
        return copies

    handed = {2: hand_over(2)}

    for a in range(4):
        for load in loads[a]:
            load.wait()
        for b in range(blocks):
            def put_slab(r, carry):
                value = jnp.concatenate([
                    waves.at[a, b, h].reshape(WAVES * STEPS, HALF)[pl.ds(r, WAVES, stride=STEPS), :] for h in range(2)
                ], 1)
                slabs[a, b * STEPS + r] = stacked(value)
                return carry

            lax.fori_loop(0, STEPS, put_slab, 0)

    def own_products(r, total):
        a = 2 - 2 * own
        total = total + dot_rows(stacked(steps_p[0, STEPS + r]), slabs[a, r])
        return total - dot_rows(stacked(steps_p[1, STEPS + r]), slabs[a + 1, r])

    def other_products(r, total):
        a = 2 * own
        total = total + dot_rows(stacked(steps_other[0, r]), slabs[a, r])
        return total - dot_rows(stacked(steps_other[1, r]), slabs[a + 1, r])

    zero = jnp.zeros((2 * RANK, HALF), F32)
    mine = lax.fori_loop(*spans[2], own_products, zero, unroll=2)
    for copy in handed[2]:
        copy.wait_recv()
    theirs = lax.fori_loop(*spans[2], other_products, zero, unroll=2)

    for copy in edges:
        copy.wait_recv()
    inside = (me > 0, me < count - 1)
    for side, row0 in enumerate((0, STEPS + ROWS)):
        put_speed(jnp.where(inside[side], speed_edges[side], 0.0), row0)
        for r in range(STEPS):
            steps_p[0, row0 + r] = rows_of(probe_edges, side, r)
    edge_sweeps(steps_p, speed, middle, beside, True)
    for index in range(2):
        handed[index] = hand_over(index)
    for index in range(2):
        mine = lax.fori_loop(*spans[index], own_products, mine, unroll=2)
    for index in range(2):
        for copy in handed[index]:
            copy.wait_recv()
        theirs = lax.fori_loop(*spans[index], other_products, theirs, unroll=2)

    def strip_sum(value, i):
        plane_send[i] = value
        copies = [
            remote(plane_send.at[i], plane_recv.at[i, d - 1], sum_send.at[i, d - 1], sum_recv.at[i, d - 1],
                   {"strip": plane_peer(d)})
            for d in range(1, PLANE)
        ]
        for copy in copies:
            copy.start()
        for d, copy in enumerate(copies):
            copy.wait_recv()
            value = value + plane_recv[i, d]
        column_send[i] = value
        more = [
            remote(column_send.at[i], column_recv.at[i, d - 1], sum_send.at[i, PLANE + d - 2],
                   sum_recv.at[i, PLANE + d - 2], {"strip": column_peer(d)})
            for d in range(1, SIDE)
        ]
        for copy in more:
            copy.start()
        for d, copy in enumerate(more):
            copy.wait_recv()
            value = value + column_recv[i, d]
        for copy in copies + more:
            copy.wait_send()
        return value

    folded = []
    for total in (mine, theirs):
        both = total[:RANK] + total[RANK:]
        folded.append(both + pltpu.roll(both, WAVES, 1))
    weight = strip_sum(jnp.where(lane < WAVES, folded[0], folded[1]), 0)
    turned = pltpu.roll(weight, WAVES, 1)
    weights[0] = stacked(jnp.where(lane < WAVES, weight, turned))
    weights[1] = stacked(jnp.where(lane < WAVES, turned, weight))

    def combine(which, level, r):
        side = away if which else own
        both = dot(weights[which], slabs[2 * side + level, r])
        return both[:RANK] + both[RANK:]

    def for_other(r, carry):
        for level in range(2):
            partial[level, r] = combine(1, level, r)
        return carry

    def for_own(r, carry):
        for level in range(2):
            fields[level, STEPS + r] = combine(0, level, r)
        return carry

    def add_arrived(r, carry):
        for level in range(2):
            fields[level, STEPS + r] = fields[level, STEPS + r] + arrived[level, r]
        return carry

    def core_copies(index):
        lo, hi = spans[index]
        copies = [
            remote(partial.at[level, pl.ds(lo, hi - lo)], arrived.at[level, pl.ds(lo, hi - lo)],
                   core_send.at[2 * index + level], core_recv.at[2 * index + level], {"shot": away})
            for level in range(2)
        ]
        for copy in copies:
            copy.start()
        return copies

    crossing = []
    for index in range(2):
        lax.fori_loop(*spans[index], for_other, 0, unroll=2)
        crossing.append(core_copies(index))
    halos = []
    for index in range(2):
        lax.fori_loop(*spans[index], for_own, 0, unroll=2)
    for index in range(2):
        for copy in crossing[index]:
            copy.wait_recv()
        lo = spans[index][0]

        def add_edge(r, carry):
            for level in range(2):
                value = fields[level, STEPS + lo + r] + arrived[level, lo + r]
                fields[level, STEPS + lo + r] = value
                leaving[index, level, r] = value
            return carry

        lax.fori_loop(0, STEPS, add_edge, 0)
        target, landing = ((before, STEPS + ROWS), (after, 0))[index]
        for level in range(2):
            at = level * index
            copy = remote(
                leaving.at[index, level, pl.ds(at, STEPS - level)],
                fields.at[level, pl.ds(landing + at, STEPS - level)],
                halo_send.at[index, level], halo_recv.at[index, level], {"strip": target},
            )
            copy.start()
            halos.append(copy)
    lax.fori_loop(*spans[2], for_other, 0, unroll=2)
    crossing.append(core_copies(2))
    lax.fori_loop(*spans[2], for_own, 0, unroll=2)
    for copy in crossing[2]:
        copy.wait_recv()
    lax.fori_loop(*spans[2], add_arrived, 0)
    inner_sweeps(fields, speed, middle, beside, False)
    for copy in halos:
        copy.wait_recv()

    for side, row0 in enumerate((0, STEPS + ROWS)):
        @pl.when(jnp.logical_not(inside[side]))
        def _():
            for level in range(2):
                for r in range(STEPS):
                    fields[level, row0 + r] = jnp.zeros((RANK, COLS), F32)

    edge_sweeps(fields, speed, middle, beside, False)

    results = [
        pltpu.make_async_copy(fields.at[0, pl.ds(STEPS, ROWS)], s_out.at[own], out_sem.at[0]),
        remote(fields.at[0, pl.ds(STEPS, ROWS)], s_out.at[own], core_send.at[6], core_recv.at[6], {"shot": away}),
    ]
    for copy in results:
        copy.start()

    def gram_rows(i, total):
        value = jnp.concatenate([stacked(fields[0, STEPS + 4 * i + j]) for j in range(4)], 1)
        return total + dot_rows(value, value)

    gram = lax.fori_loop(0, ROWS // 4, gram_rows, jnp.zeros((2 * RANK, 2 * RANK), F32))
    gram = gram[:RANK] + gram[RANK:]
    gram = gram[:, :RANK] + gram[:, RANK:]
    gram = strip_sum(jnp.concatenate([gram, jnp.zeros((RANK, HALF - RANK), F32)], 1), 1)
    plane_send[2] = gram
    swap = remote(plane_send.at[2], other_gram, core_send.at[7], core_recv.at[7], {"shot": away})
    swap.start()
    swap.wait()
    theirs = other_gram[...]
    flag = (own + jnp.zeros((RANK, HALF), jnp.int32)) == 0
    inv_out[0] = lower_inverse(jnp.where(flag, gram, theirs))
    inv_out[1] = lower_inverse(jnp.where(flag, theirs, gram))

    for copy in results:
        copy.wait()
    for copy in edges + halos:
        copy.wait_send()
    for copies in crossing + list(handed.values()):
        for copy in copies:
            copy.wait_send()


def final_kernel(scale, s_hbm, inv_ref, left_out, right_out, sketch, blocks, load_sem, sem):
    count = ROWS // STEPS
    loads = {}
    for b in range(count):
        for side in range(2):
            loads[b, side] = pltpu.make_async_copy(
                s_hbm.at[side, pl.ds(b * STEPS, STEPS)], sketch.at[side, b], load_sem.at[side, b]
            )
            loads[b, side].start()
    lhs = []
    for side in range(2):
        high, low = split((inv_ref[side] * scale)[:, RANK : 2 * RANK])
        lhs.append(jnp.concatenate([jnp.concatenate([high, high], 1), jnp.concatenate([low, low], 1)], 0))
    copies = []
    for b in range(count):
        for side, out in enumerate((left_out, right_out)):
            loads[b, side].wait()
            for r in range(STEPS):
                both = dot(lhs[side], stacked(sketch[side, b, r]))
                value = both[:RANK] + both[RANK:]
                for h in range(2):
                    blocks.at[side, b, h].reshape(RANK * STEPS, HALF)[pl.ds(r, RANK, stride=STEPS), :] = (
                        value[:, h * HALF : (h + 1) * HALF]
                    )
            for h in range(2):
                copy = pltpu.make_async_copy(
                    blocks.at[side, b, h],
                    out.at[:, pl.ds(b * STEPS, STEPS), pl.ds(h * HALF, HALF)],
                    sem.at[side, b, h],
                )
                copy.start()
                copies.append(copy)
    for copy in copies:
        copy.wait()


def shards(source_now, source_prev, adjoint_now, adjoint_prev, courant, probe_left, probe_right):
    waves = [a.reshape(WAVES, ROWS, COLS) for a in (source_now, source_prev, adjoint_now, adjoint_prev)]
    any_spec = pl.BlockSpec(memory_space=pl.ANY)
    vmem_spec = pl.BlockSpec(memory_space=pltpu.VMEM)
    dma = pltpu.SemaphoreType.DMA
    count = ROWS // STEPS
    sketch, inverse = pl.pallas_call(
        main_kernel,
        out_shape=(
            jax.ShapeDtypeStruct((2, ROWS, RANK, COLS), F32),
            jax.ShapeDtypeStruct((2, RANK, HALF), F32),
        ),
        in_specs=[any_spec] * 7,
        out_specs=(any_spec, vmem_spec),
        scratch_shapes=[
            pltpu.VMEM((4, count, 2, WAVES, STEPS, HALF), F32),
            pltpu.VMEM((4, ROWS, 2 * WAVES, COLS), BF16),
            pltpu.VMEM((count, 2, RANK, STEPS, HALF), F32),
            pltpu.VMEM((2, 2, RANK, STEPS, HALF), F32),
            pltpu.VMEM((ROWS, COLS), F32),
            pltpu.VMEM((2, STEPS, COLS), F32),
            pltpu.VMEM((TALL, 8, COLS), F32),
            pltpu.VMEM((TALL, 8, COLS), F32),
            pltpu.VMEM((COLS, COLS), BF16),
            pltpu.VMEM((2, TALL, RANK, COLS), F32),
            pltpu.VMEM((2, ROWS, RANK, COLS), F32),
            pltpu.VMEM((2, 2 * RANK, HALF), BF16),
            pltpu.VMEM((3, RANK, HALF), F32),
            pltpu.VMEM((2, PLANE - 1, RANK, HALF), F32),
            pltpu.VMEM((2, RANK, HALF), F32),
            pltpu.VMEM((2, SIDE - 1, RANK, HALF), F32),
            pltpu.VMEM((RANK, HALF), F32),
            pltpu.VMEM((2, TALL, RANK, COLS), F32),
            pltpu.VMEM((2, 2, STEPS, RANK, COLS), F32),
            pltpu.VMEM((2, ROWS, RANK, COLS), F32),
            pltpu.VMEM((2, ROWS, RANK, COLS), F32),
            dma((1 + 2 * count + 8 * count,)),
            dma((2, 3)),
            dma((2, 3)),
            dma((2, PLANE + SIDE - 2)),
            dma((2, PLANE + SIDE - 2)),
            dma((8,)),
            dma((8,)),
            dma((2, 2)),
            dma((2, 2)),
            dma((3, 2)),
            dma((3, 2)),
            dma((1,)),
        ],
        compiler_params=pltpu.CompilerParams(
            collective_id=0, has_side_effects=True, vmem_limit_bytes=56 * 1024 * 1024
        ),
        name="sketch",
    )(*waves, courant, probe_left, probe_right)
    scale = math.sqrt(ROWS * lax.axis_size("strip") * COLS)
    return pl.pallas_call(
        functools.partial(final_kernel, scale),
        out_shape=(jax.ShapeDtypeStruct((RANK, ROWS, COLS), F32),) * 2,
        in_specs=[any_spec, vmem_spec],
        out_specs=(any_spec, any_spec),
        scratch_shapes=[
            pltpu.VMEM((2, count, STEPS, RANK, COLS), F32),
            pltpu.VMEM((2, count, 2, RANK, STEPS, HALF), F32),
            dma((2, count)),
            dma((2, count, 2)),
        ],
        name="factors",
    )(sketch, inverse)


def solution(mesh):
    return jax.shard_map(
        shards,
        mesh=mesh,
        in_specs=(P("shot", None, "strip", None),) * 4 + (P("strip", None),) + (P(None, "strip", None),) * 2,
        out_specs=(P(None, "strip", None), P(None, "strip", None)),
        check_vma=False,
    )
```

```python
import functools
import math

import jax
import jax.numpy as jnp
from jax import lax
from jax.experimental import pallas as pl
from jax.experimental.pallas import tpu as pltpu
from jax.sharding import PartitionSpec as P

STEPS = 8
WAVES = 64
RANK = 16
ROWS = 32
COLS = 256
HALF = 128
TALL = ROWS + 2 * STEPS
SIDE = 4
PLANE = SIDE * SIDE
MESH = pl.DeviceIdType.MESH


def hops(d):
    return sum(min(k, SIDE - k) for k in (d % SIDE, d // SIDE))


FAR_FIRST = sorted(range(1, PLANE), key=lambda d: -hops(d))
COLUMN_FIRST = (2, 1, 3)
F32 = jnp.float32
BF16 = jnp.bfloat16


def split(x):
    high = x.astype(BF16)
    low = (x - high.astype(F32)).astype(BF16)
    return high, low


def stacked(x):
    return jnp.concatenate(split(x), 0)


def dot_rows(a, b):
    return lax.dot_general(a, b, (((1,), (1,)), ((), ())), preferred_element_type=F32)


def dot(a, b):
    return lax.dot_general(a, b, (((1,), (0,)), ((), ())), preferred_element_type=F32)


def spread_of(cells, beside):
    count = cells.shape[0]
    both = dot(jnp.concatenate(split(cells.reshape(count * RANK, COLS)), 0), beside[...])
    return (both[: count * RANK] + both[count * RANK :]).reshape(count, 2, 8, COLS)


def load_rows(ref, low, count):
    return ref[pl.ds(low, count)].reshape(count, 2, 8, COLS)


def advance(buf, speed, middle, beside, level, starts, count, transposed):
    now = buf.at[lax.rem(level + 1, 2)]
    new = buf.at[lax.rem(level, 2)]
    pieces = []
    for low in starts:
        cells = load_rows(now, low - 1, count + 2)
        if transposed:
            cells = cells * speed[pl.ds(low - 1, count + 2)][:, None]
        pieces.append(cells)
    inner = [cells[1:-1] for cells in pieces]
    side = spread_of(inner[0] if len(inner) == 1 else jnp.concatenate(inner, 0), beside)
    for k, low in enumerate(starts):
        total = pieces[k][:-2] + pieces[k][2:] + side[k * count : (k + 1) * count]
        if not transposed:
            total = total * speed[pl.ds(low, count)][:, None]
        centre = load_rows(now, low, count) if transposed else inner[k]
        value = middle[pl.ds(low, count)][:, None] * centre - load_rows(new, low, count) + total
        new[pl.ds(low, count)] = value.reshape(count, RANK, COLS)


def inner_sweeps(buf, speed, middle, beside, transposed):
    for level in range(1, STEPS + 1):
        advance(buf, speed, middle, beside, level, (STEPS + level,), ROWS - 2 * level, transposed)


def edge_sweeps(buf, speed, middle, beside, transposed):
    def body(level, carry):
        advance(buf, speed, middle, beside, level, (level, STEPS + ROWS - level), STEPS, transposed)
        return carry

    lax.fori_loop(1, STEPS + 1, body, 0)


def lower_inverse(gram):
    row = lax.broadcasted_iota(jnp.int32, (RANK, HALF), 0)
    lane = lax.broadcasted_iota(jnp.int32, (RANK, HALF), 1)
    work = jnp.where(lane < RANK, gram, jnp.where(lane == row + RANK, 1.0, 0.0))
    for k in range(RANK):
        pivot = work[k : k + 1, k : k + 1]
        root = 1.0 / jnp.sqrt(pivot)
        line = work[k : k + 1, :] * root
        column = jnp.where(row[:, :1] > k, work[:, k : k + 1] * root, 0.0)
        work = jnp.where(row == k, line, work - column * line)
    return work


def main_kernel(
    scale, src_now, src_prev, adj_now, adj_prev, courant, probe_left, probe_right,
    left_out, right_out,
    waves, slabs, probes, probe_edges, speed_own, speed_edges, speed, middle, beside,
    steps_p, steps_other, weights, plane_send, plane_recv, column_send, column_recv, gram_send, gram_recv, pair_send, pair_recv, sketches, inverses,
    fields, leaving, partial, arrived,
    load_sem, edge_send, edge_recv, sum_send, sum_recv, core_send, core_recv, halo_send, halo_recv,
    step_send, step_recv, keep_sem,
):
    own = lax.axis_index("shot")
    away = 1 - own
    me = lax.axis_index("strip")
    count = lax.axis_size("strip")
    x, y, z = me % SIDE, (me // SIDE) % SIDE, me // PLANE
    after, before = (me + 1) % count, (me + count - 1) % count
    lane = lax.broadcasted_iota(jnp.int32, (RANK, HALF), 1)
    blocks = ROWS // STEPS
    targets = ((after, ROWS - STEPS), (before, 0))
    halves = [pl.ds(0, HALF), pl.ds(HALF, HALF)]

    def plane_peer(d):
        return z * PLANE + ((y + d // SIDE) % SIDE) * SIDE + (x + d % SIDE) % SIDE

    def column_peer(d):
        return ((z + d) % SIDE) * PLANE + y * SIDE + x

    def remote(src, dst, send, recv, device):
        return pltpu.make_async_remote_copy(
            src_ref=src, dst_ref=dst, send_sem=send, recv_sem=recv, device_id=device, device_id_type=MESH
        )

    barrier = pltpu.get_barrier_semaphore()
    strips = [after, before] + [plane_peer(d) for d in FAR_FIRST] + [column_peer(d) for d in COLUMN_FIRST]
    for peer in strips:
        pl.semaphore_signal(barrier, inc=1, device_id={"strip": peer}, device_id_type=MESH)
    pl.semaphore_signal(barrier, inc=1, device_id={"shot": away}, device_id_type=MESH)
    for d in FAR_FIRST:
        pl.semaphore_signal(barrier, inc=1, device_id={"strip": plane_peer(d), "shot": away}, device_id_type=MESH)

    def probe_loads(probe):
        return [
            pltpu.make_async_copy(probe.at[:, pl.ds(b * STEPS, STEPS), halves[h]], probes.at[b, h], load_sem.at[1 + 2 * b + h])
            for b in range(blocks)
            for h in range(2)
        ]

    def probe_sends(probe):
        return [
            remote(probe.at[:, pl.ds(first, STEPS), halves[h]], probe_edges.at[side, h],
                   edge_send.at[side, 1 + h], edge_recv.at[side, 1 + h], {"strip": target})
            for side, (target, first) in enumerate(targets)
            for h in range(2)
        ]

    load_speed = pltpu.make_async_copy(courant, speed_own, load_sem.at[0])
    load_speed.start()
    for core, probe in enumerate((probe_left, probe_right)):
        @pl.when(own == core)
        def _():
            for load in probe_loads(probe):
                load.start()
    base = 1 + 2 * blocks
    loads = [
        [
            pltpu.make_async_copy(
                wave.at[:, pl.ds(b * STEPS, STEPS), halves[h]], waves.at[a, b, h],
                load_sem.at[base + (a * blocks + b) * 2 + h],
            )
            for b in range(blocks)
            for h in range(2)
        ]
        for a, wave in enumerate((src_now, src_prev, adj_now, adj_prev))
    ]
    for group in loads:
        for load in group:
            load.start()

    near = lax.broadcasted_iota(jnp.int32, (COLS, COLS), 0) - lax.broadcasted_iota(jnp.int32, (COLS, COLS), 1)
    beside[...] = jnp.where(jnp.abs(near) == 1, 1.0, 0.0).astype(BF16)

    def put_speed(values, row0):
        for r in range(STEPS):
            value = jnp.broadcast_to(values[r : r + 1, :], (8, COLS))
            speed[row0 + r] = value
            middle[row0 + r] = 2.0 - 4.0 * value

    load_speed.wait()
    for block in range(blocks):
        put_speed(speed_own[pl.ds(block * STEPS, STEPS), :], STEPS + block * STEPS)
    for load in probe_loads(probe_left):
        load.wait()

    def rows_of(tiles, b, r):
        return jnp.concatenate([
            tiles.at[b, h].reshape(RANK * STEPS, HALF)[pl.ds(r, RANK, stride=STEPS), :] for h in range(2)
        ], 1)

    for b in range(blocks):
        for r in range(STEPS):
            steps_p[0, STEPS + b * STEPS + r] = rows_of(probes, b, r)

    def put_zero(r, carry):
        steps_p[1, r] = jnp.zeros((RANK, COLS), F32)
        return carry

    lax.fori_loop(0, TALL, put_zero, 0)

    pl.semaphore_wait(barrier, len(strips) + PLANE)

    speed_sends = [
        remote(courant.at[pl.ds(first, STEPS)], speed_edges.at[side],
               edge_send.at[side, 0], edge_recv.at[side, 0], {"strip": target})
        for side, (target, first) in enumerate(targets)
    ]
    for copy in speed_sends:
        copy.start()
    for core, probe in enumerate((probe_left, probe_right)):
        @pl.when(own == core)
        def _():
            for copy in probe_sends(probe):
                copy.start()
    edges = speed_sends + probe_sends(probe_left)

    inner_sweeps(steps_p, speed, middle, beside, True)

    spans = ((0, STEPS), (ROWS - STEPS, ROWS), (STEPS, ROWS - STEPS))

    def hand_over(index):
        lo, hi = spans[index]
        copies = [
            remote(steps_p.at[level, pl.ds(STEPS + lo, hi - lo)], steps_other.at[level, pl.ds(lo, hi - lo)],
                   step_send.at[index, level], step_recv.at[index, level], {"shot": away})
            for level in range(2)
        ]
        for copy in copies:
            copy.start()
        return copies

    handed = {2: hand_over(2)}

    for a in range(4):
        for load in loads[a]:
            load.wait()
        for b in range(blocks):
            def put_slab(r, carry):
                value = jnp.concatenate([
                    waves.at[a, b, h].reshape(WAVES * STEPS, HALF)[pl.ds(r, WAVES, stride=STEPS), :] for h in range(2)
                ], 1)
                slabs[a, b * STEPS + r] = stacked(value)
                return carry

            lax.fori_loop(0, STEPS, put_slab, 0)

    def own_products(r, total):
        a = 2 - 2 * own
        total = total + dot_rows(stacked(steps_p[0, STEPS + r]), slabs[a, r])
        return total - dot_rows(stacked(steps_p[1, STEPS + r]), slabs[a + 1, r])

    def other_products(r, total):
        a = 2 * own
        total = total + dot_rows(stacked(steps_other[0, r]), slabs[a, r])
        return total - dot_rows(stacked(steps_other[1, r]), slabs[a + 1, r])

    zero = jnp.zeros((2 * RANK, HALF), F32)
    mine = lax.fori_loop(*spans[2], own_products, zero, unroll=4)

    for copy in edges:
        copy.wait_recv()
    inside = (me > 0, me < count - 1)
    for side, row0 in enumerate((0, STEPS + ROWS)):
        put_speed(jnp.where(inside[side], speed_edges[side], 0.0), row0)
        for r in range(STEPS):
            steps_p[0, row0 + r] = rows_of(probe_edges, side, r)
    edge_sweeps(steps_p, speed, middle, beside, True)
    for index in range(2):
        handed[index] = hand_over(index)
    for copy in handed[2]:
        copy.wait_recv()
    theirs = lax.fori_loop(*spans[2], other_products, zero, unroll=4)
    for index in range(2):
        mine = lax.fori_loop(*spans[index], own_products, mine, unroll=4)
    for index in range(2):
        for copy in handed[index]:
            copy.wait_recv()
        theirs = lax.fori_loop(*spans[index], other_products, theirs, unroll=4)

    def start(src, dst, k, device):
        copy = remote(src, dst, sum_send.at[k], sum_recv.at[k], device)
        copy.start()
        return copy

    def strip_sum(value):
        plane_send[...] = value
        copies = {d: start(plane_send, plane_recv.at[d - 1], d - 1, {"strip": plane_peer(d)}) for d in FAR_FIRST}
        for d in range(1, PLANE):
            copies[d].wait_recv()
            value = value + plane_recv[d - 1]
        column_send[...] = value
        more = {
            d: start(column_send, column_recv.at[d - 1], PLANE + d - 2, {"strip": column_peer(d)}) for d in COLUMN_FIRST
        }
        for d in range(1, SIDE):
            more[d].wait_recv()
            value = value + column_recv[d - 1]
        for copy in list(copies.values()) + list(more.values()):
            copy.wait_send()
        return value

    def gram_sum(value):
        first = PLANE + SIDE - 2
        gram_send[...] = value
        copies = {}
        for d in FAR_FIRST:
            copies[0, d] = start(gram_send, gram_recv.at[0, d], first + d, {"strip": plane_peer(d)})
            copies[1, d] = start(gram_send, gram_recv.at[1, d], first + PLANE + d, {"strip": plane_peer(d), "shot": away})
        copies[1, 0] = start(gram_send, gram_recv.at[1, 0], first + PLANE, {"shot": away})
        for d in range(1, PLANE):
            copies[0, d].wait_recv()
            value = value + gram_recv[0, d]
        copies[1, 0].wait_recv()
        other = gram_recv[1, 0]
        for d in range(1, PLANE):
            copies[1, d].wait_recv()
            other = other + gram_recv[1, d]
        pair = [value, other]
        for k in range(2):
            pair_send[k] = pair[k]
        more = {}
        for d in COLUMN_FIRST:
            more[d] = start(pair_send, pair_recv.at[d - 1], first + 2 * PLANE + d - 1, {"strip": column_peer(d)})
        for d in range(1, SIDE):
            more[d].wait_recv()
            pair = [pair[k] + pair_recv[d - 1, k] for k in range(2)]
        for copy in list(copies.values()) + list(more.values()):
            copy.wait_send()
        return pair

    folded = []
    for total in (mine, theirs):
        both = total[:RANK] + total[RANK:]
        folded.append(both + pltpu.roll(both, WAVES, 1))
    weight = strip_sum(jnp.where(lane < WAVES, folded[0], folded[1]))
    turned = pltpu.roll(weight, WAVES, 1)
    weights[0] = stacked(jnp.where(lane < WAVES, weight, turned))
    weights[1] = stacked(jnp.where(lane < WAVES, turned, weight))

    def combine(which, level, r):
        side = away if which else own
        both = dot(weights[which], slabs[2 * side + level, r])
        return both[:RANK] + both[RANK:]

    def for_other(level, r, carry):
        partial[level, r] = combine(1, level, r)
        return carry

    def for_own(level, r, carry):
        fields[level, STEPS + r] = combine(0, level, r)
        return carry

    def cross(level, index):
        lo, hi = spans[index]
        copy = remote(
            partial.at[level, pl.ds(lo, hi - lo)], arrived.at[level, pl.ds(lo, hi - lo)],
            core_send.at[2 * index + level], core_recv.at[2 * index + level], {"shot": away},
        )
        copy.start()
        return copy

    crossing = {}
    for level in range(2):
        for index in range(2):
            lax.fori_loop(*spans[index], functools.partial(for_other, level), 0, unroll=8)
            crossing[level, index] = cross(level, index)
    halos = []
    for level in range(2):
        for index in range(2):
            lax.fori_loop(*spans[index], functools.partial(for_own, level), 0, unroll=8)
            crossing[level, index].wait_recv()
            lo, hi = spans[index]
            value = fields[level, STEPS + lo : STEPS + hi] + arrived[level, lo:hi]
            fields[level, STEPS + lo : STEPS + hi] = value
            leaving[index, level] = value
            target, landing = ((before, STEPS + ROWS), (after, 0))[index]
            at = level * index
            copy = remote(
                leaving.at[index, level, pl.ds(at, STEPS - level)],
                fields.at[level, pl.ds(landing + at, STEPS - level)],
                halo_send.at[index, level], halo_recv.at[index, level], {"strip": target},
            )
            copy.start()
            halos.append(copy)
    for level in range(2):
        lax.fori_loop(*spans[2], functools.partial(for_other, level), 0, unroll=4)
        crossing[level, 2] = cross(level, 2)
    for level in range(2):
        lax.fori_loop(*spans[2], functools.partial(for_own, level), 0, unroll=4)
    for level in range(2):
        crossing[level, 2].wait_recv()
        lo, hi = spans[2]
        fields[level, STEPS + lo : STEPS + hi] = fields[level, STEPS + lo : STEPS + hi] + arrived[level, lo:hi]
    inner_sweeps(fields, speed, middle, beside, False)
    for copy in halos:
        copy.wait_recv()

    for side, row0 in enumerate((0, STEPS + ROWS)):
        @pl.when(jnp.logical_not(inside[side]))
        def _():
            for level in range(2):
                for r in range(STEPS):
                    fields[level, row0 + r] = jnp.zeros((RANK, COLS), F32)

    edge_sweeps(fields, speed, middle, beside, False)

    crossed = remote(
        fields.at[0, pl.ds(STEPS, ROWS)], sketches.at[own], core_send.at[6], core_recv.at[6], {"shot": away}
    )
    crossed.start()
    kept = pltpu.make_async_copy(fields.at[0, pl.ds(STEPS, ROWS)], sketches.at[own], keep_sem.at[0])
    kept.start()

    gram = jnp.zeros((2 * RANK, 2 * RANK), F32)
    for i in range(ROWS // 4):
        value = jnp.concatenate([stacked(fields[0, STEPS + 4 * i + j]) for j in range(4)], 1)
        gram = gram + dot_rows(value, value)
    gram = gram[:RANK] + gram[RANK:]
    gram = gram[:, :RANK] + gram[:, RANK:]
    packed = jnp.concatenate([gram[:8], gram[8:], jnp.zeros((8, HALF - 2 * RANK), F32)], 1)
    for side, packed in zip((own, away), gram_sum(packed)):
        gram = jnp.concatenate([packed, pltpu.roll(packed, HALF - RANK, 1)], 0)
        high, low = split(lower_inverse(gram) * scale)
        inverses[side, 0] = high
        inverses[side, 1] = low
    crossed.wait_recv()
    kept.wait()
    for side, out in enumerate((left_out, right_out)):
        high, low = (inverses[side, k][:, RANK : 2 * RANK] for k in range(2))
        lhs = jnp.concatenate([jnp.concatenate([high, high], 1), jnp.concatenate([low, low], 1)], 0)

        def put_block(b, carry):
            for r in range(STEPS):
                both = dot(lhs, stacked(sketches[side, b * STEPS + r]))
                value = both[:RANK] + both[RANK:]
                for h in range(2):
                    out.at[b, h].reshape(RANK * STEPS, HALF)[pl.ds(r, RANK, stride=STEPS), :] = (
                        value[:, h * HALF : (h + 1) * HALF]
                    )
            return carry

        lax.fori_loop(0, blocks, put_block, 0)

    crossed.wait_send()
    for copy in edges + halos:
        copy.wait_send()
    for copy in crossing.values():
        copy.wait_send()
    for copies in handed.values():
        for copy in copies:
            copy.wait_send()


def shards(source_now, source_prev, adjoint_now, adjoint_prev, courant, probe_left, probe_right):
    waves = [a.reshape(WAVES, ROWS, COLS) for a in (source_now, source_prev, adjoint_now, adjoint_prev)]
    any_spec = pl.BlockSpec(memory_space=pl.ANY)
    vmem_spec = pl.BlockSpec(memory_space=pltpu.VMEM)
    dma = pltpu.SemaphoreType.DMA
    count = ROWS // STEPS
    scale = math.sqrt(ROWS * lax.axis_size("strip") * COLS)
    factors = pl.pallas_call(
        functools.partial(main_kernel, scale),
        out_shape=(pltpu.VMEM((count, 2, RANK, STEPS, HALF), F32),) * 2,
        in_specs=[any_spec] * 7,
        out_specs=(vmem_spec, vmem_spec),
        scratch_shapes=[
            pltpu.VMEM((4, count, 2, WAVES, STEPS, HALF), F32),
            pltpu.VMEM((4, ROWS, 2 * WAVES, COLS), BF16),
            pltpu.VMEM((count, 2, RANK, STEPS, HALF), F32),
            pltpu.VMEM((2, 2, RANK, STEPS, HALF), F32),
            pltpu.VMEM((ROWS, COLS), F32),
            pltpu.VMEM((2, STEPS, COLS), F32),
            pltpu.VMEM((TALL, 8, COLS), F32),
            pltpu.VMEM((TALL, 8, COLS), F32),
            pltpu.VMEM((COLS, COLS), BF16),
            pltpu.VMEM((2, TALL, RANK, COLS), F32),
            pltpu.VMEM((2, ROWS, RANK, COLS), F32),
            pltpu.VMEM((2, 2 * RANK, HALF), BF16),
            pltpu.VMEM((RANK, HALF), F32),
            pltpu.VMEM((PLANE - 1, RANK, HALF), F32),
            pltpu.VMEM((RANK, HALF), F32),
            pltpu.VMEM((SIDE - 1, RANK, HALF), F32),
            pltpu.VMEM((8, HALF), F32),
            pltpu.VMEM((2, PLANE, 8, HALF), F32),
            pltpu.VMEM((2, 8, HALF), F32),
            pltpu.VMEM((SIDE - 1, 2, 8, HALF), F32),
            pltpu.VMEM((2, ROWS, RANK, COLS), F32),
            pltpu.VMEM((2, 2, RANK, HALF), BF16),
            pltpu.VMEM((2, TALL, RANK, COLS), F32),
            pltpu.VMEM((2, 2, STEPS, RANK, COLS), F32),
            pltpu.VMEM((2, ROWS, RANK, COLS), F32),
            pltpu.VMEM((2, ROWS, RANK, COLS), F32),
            dma((1 + 2 * count + 8 * count,)),
            dma((2, 3)),
            dma((2, 3)),
            dma((3 * PLANE + 2 * SIDE - 3,)),
            dma((3 * PLANE + 2 * SIDE - 3,)),
            dma((8,)),
            dma((8,)),
            dma((2, 2)),
            dma((2, 2)),
            dma((3, 2)),
            dma((3, 2)),
            dma((1,)),
        ],
        compiler_params=pltpu.CompilerParams(
            collective_id=0, has_side_effects=True, vmem_limit_bytes=56 * 1024 * 1024
        ),
        name="sketch",
    )(*waves, courant, probe_left, probe_right)
    return tuple(factor.transpose(2, 0, 3, 1, 4).reshape(RANK, ROWS, COLS) for factor in factors)


def solution(mesh):
    return jax.shard_map(
        shards,
        mesh=mesh,
        in_specs=(P("shot", None, "strip", None),) * 4 + (P("strip", None),) + (P(None, "strip", None),) * 2,
        out_specs=(P(None, "strip", None), P(None, "strip", None)),
        check_vma=False,
    )
```

```python
import functools
import math

import jax
import jax.numpy as jnp
from jax import lax
from jax.experimental import pallas as pl
from jax.experimental.pallas import tpu as pltpu
from jax.sharding import PartitionSpec as P

STEPS = 8
WAVES = 64
RANK = 16
ROWS = 32
COLS = 256
HALF = 128
TALL = ROWS + 2 * STEPS
SIDE = 4
PLANE = SIDE * SIDE
MESH = pl.DeviceIdType.MESH


def hops(d):
    return sum(min(k, SIDE - k) for k in (d % SIDE, d // SIDE))


FAR_FIRST = sorted(range(1, PLANE), key=lambda d: -hops(d))
COLUMN_FIRST = (2, 1, 3)
F32 = jnp.float32
BF16 = jnp.bfloat16


def split(x):
    high = x.astype(BF16)
    low = (x - high.astype(F32)).astype(BF16)
    return high, low


def stacked(x):
    return jnp.concatenate(split(x), 0)


def dot_rows(a, b):
    return lax.dot_general(a, b, (((1,), (1,)), ((), ())), preferred_element_type=F32)


def dot(a, b):
    return lax.dot_general(a, b, (((1,), (0,)), ((), ())), preferred_element_type=F32)


def spread_of(cells, beside):
    count = cells.shape[0]
    both = dot(jnp.concatenate(split(cells.reshape(count * RANK, COLS)), 0), beside[...])
    return (both[: count * RANK] + both[count * RANK :]).reshape(count, 2, 8, COLS)


def load_rows(ref, low, count):
    return ref[pl.ds(low, count)].reshape(count, 2, 8, COLS)


def advance(buf, speed, middle, beside, level, starts, count, transposed):
    now = buf.at[lax.rem(level + 1, 2)]
    new = buf.at[lax.rem(level, 2)]
    pieces = []
    for low in starts:
        cells = load_rows(now, low - 1, count + 2)
        if transposed:
            cells = cells * speed[pl.ds(low - 1, count + 2)][:, None]
        pieces.append(cells)
    inner = [cells[1:-1] for cells in pieces]
    side = spread_of(inner[0] if len(inner) == 1 else jnp.concatenate(inner, 0), beside)
    for k, low in enumerate(starts):
        total = pieces[k][:-2] + pieces[k][2:] + side[k * count : (k + 1) * count]
        if not transposed:
            total = total * speed[pl.ds(low, count)][:, None]
        centre = load_rows(now, low, count) if transposed else inner[k]
        value = middle[pl.ds(low, count)][:, None] * centre - load_rows(new, low, count) + total
        new[pl.ds(low, count)] = value.reshape(count, RANK, COLS)


def inner_sweeps(buf, speed, middle, beside, transposed):
    for level in range(1, STEPS + 1):
        advance(buf, speed, middle, beside, level, (STEPS + level,), ROWS - 2 * level, transposed)


def edge_sweeps(buf, speed, middle, beside, transposed):
    def body(level, carry):
        advance(buf, speed, middle, beside, level, (level, STEPS + ROWS - level), STEPS, transposed)
        return carry

    lax.fori_loop(1, STEPS + 1, body, 0)


def lower_inverse(gram):
    row = lax.broadcasted_iota(jnp.int32, (RANK, HALF), 0)
    lane = lax.broadcasted_iota(jnp.int32, (RANK, HALF), 1)
    work = jnp.where(lane < RANK, gram, jnp.where(lane == row + RANK, 1.0, 0.0))
    for k in range(RANK):
        pivot = work[k : k + 1, k : k + 1]
        root = lax.rsqrt(pivot)
        line = work[k : k + 1, :] * root
        column = jnp.where(row[:, :1] > k, work[:, k : k + 1] * root, 0.0)
        work = jnp.where(row == k, line, work - column * line)
    return work


def main_kernel(
    scale, src_now, src_prev, adj_now, adj_prev, courant, probe_left, probe_right,
    left_out, right_out,
    waves, slabs, probes, probe_edges, speed_own, speed_edges, speed, middle, beside,
    steps_p, steps_other, weights, plane_send, plane_recv, column_send, column_recv, gram_send, gram_recv, pair_send, pair_recv, sketches, inverses,
    fields, leaving, partial, arrived,
    load_sem, edge_send, edge_recv, sum_send, sum_recv, core_send, core_recv, halo_send, halo_recv,
    step_send, step_recv, keep_sem,
):
    own = lax.axis_index("shot")
    away = 1 - own
    me = lax.axis_index("strip")
    count = lax.axis_size("strip")
    x, y, z = me % SIDE, (me // SIDE) % SIDE, me // PLANE
    after, before = (me + 1) % count, (me + count - 1) % count
    lane = lax.broadcasted_iota(jnp.int32, (RANK, HALF), 1)
    blocks = ROWS // STEPS
    targets = ((after, ROWS - STEPS), (before, 0))
    halves = [pl.ds(0, HALF), pl.ds(HALF, HALF)]

    def plane_peer(d):
        return z * PLANE + ((y + d // SIDE) % SIDE) * SIDE + (x + d % SIDE) % SIDE

    def column_peer(d):
        return ((z + d) % SIDE) * PLANE + y * SIDE + x

    def remote(src, dst, send, recv, device):
        return pltpu.make_async_remote_copy(
            src_ref=src, dst_ref=dst, send_sem=send, recv_sem=recv, device_id=device, device_id_type=MESH
        )

    barrier = pltpu.get_barrier_semaphore()
    inside = (me > 0, me < count - 1)
    for side, peer in enumerate((before, after)):
        @pl.when(inside[side])
        def _():
            pl.semaphore_signal(barrier, inc=1, device_id={"strip": peer}, device_id_type=MESH)
    strips = [plane_peer(d) for d in FAR_FIRST] + [column_peer(d) for d in COLUMN_FIRST]
    for peer in strips:
        pl.semaphore_signal(barrier, inc=1, device_id={"strip": peer}, device_id_type=MESH)
    pl.semaphore_signal(barrier, inc=1, device_id={"shot": away}, device_id_type=MESH)
    for d in FAR_FIRST:
        pl.semaphore_signal(barrier, inc=1, device_id={"strip": plane_peer(d), "shot": away}, device_id_type=MESH)

    def probe_loads(probe):
        return [
            pltpu.make_async_copy(probe.at[:, pl.ds(b * STEPS, STEPS), halves[h]], probes.at[b, h], load_sem.at[1 + 2 * b + h])
            for b in range(blocks)
            for h in range(2)
        ]

    def probe_sends(probe, side):
        target, first = targets[side]
        return [
            remote(probe.at[:, pl.ds(first, STEPS), halves[h]], probe_edges.at[side, h],
                   edge_send.at[side, 1 + h], edge_recv.at[side, 1 + h], {"strip": target})
            for h in range(2)
        ]

    load_speed = pltpu.make_async_copy(courant, speed_own, load_sem.at[0])
    load_speed.start()
    for core, probe in enumerate((probe_left, probe_right)):
        @pl.when(own == core)
        def _():
            for load in probe_loads(probe):
                load.start()
    base = 1 + 2 * blocks
    loads = [
        [
            pltpu.make_async_copy(
                wave.at[:, pl.ds(b * STEPS, STEPS), halves[h]], waves.at[a, b, h],
                load_sem.at[base + (a * blocks + b) * 2 + h],
            )
            for b in range(blocks)
            for h in range(2)
        ]
        for a, wave in enumerate((src_now, src_prev, adj_now, adj_prev))
    ]
    for group in loads:
        for load in group:
            load.start()

    pl.semaphore_wait(barrier, len(strips) + PLANE + sum(flag.astype(jnp.int32) for flag in inside))

    speed_sends = [
        remote(courant.at[pl.ds(first, STEPS)], speed_edges.at[side],
               edge_send.at[side, 0], edge_recv.at[side, 0], {"strip": target})
        for side, (target, first) in enumerate(targets)
    ]
    for side in range(2):
        @pl.when(inside[1 - side])
        def _():
            speed_sends[side].start()
        for core, probe in enumerate((probe_left, probe_right)):
            @pl.when(jnp.logical_and(inside[1 - side], own == core))
            def _():
                for copy in probe_sends(probe, side):
                    copy.start()
    edges = [[speed_sends[side]] + probe_sends(probe_left, side) for side in range(2)]

    near = lax.broadcasted_iota(jnp.int32, (COLS, COLS), 0) - lax.broadcasted_iota(jnp.int32, (COLS, COLS), 1)
    beside[...] = jnp.where(jnp.abs(near) == 1, 1.0, 0.0).astype(BF16)

    def put_speed(values, row0):
        for r in range(STEPS):
            value = jnp.broadcast_to(values[r : r + 1, :], (8, COLS))
            speed[row0 + r] = value
            middle[row0 + r] = 2.0 - 4.0 * value

    load_speed.wait()
    for block in range(blocks):
        put_speed(speed_own[pl.ds(block * STEPS, STEPS), :], STEPS + block * STEPS)
    for load in probe_loads(probe_left):
        load.wait()

    def rows_of(tiles, b, r):
        return jnp.concatenate([
            tiles.at[b, h].reshape(RANK * STEPS, HALF)[pl.ds(r, RANK, stride=STEPS), :] for h in range(2)
        ], 1)

    for b in range(blocks):
        for r in range(STEPS):
            steps_p[0, STEPS + b * STEPS + r] = rows_of(probes, b, r)

    def put_zero(r, carry):
        steps_p[1, r] = jnp.zeros((RANK, COLS), F32)
        return carry

    lax.fori_loop(0, TALL, put_zero, 0)

    inner_sweeps(steps_p, speed, middle, beside, True)

    spans = ((0, STEPS), (ROWS - STEPS, ROWS), (STEPS, ROWS - STEPS))

    def hand_over(index):
        lo, hi = spans[index]
        copies = [
            remote(steps_p.at[level, pl.ds(STEPS + lo, hi - lo)], steps_other.at[level, pl.ds(lo, hi - lo)],
                   step_send.at[index, level], step_recv.at[index, level], {"shot": away})
            for level in range(2)
        ]
        for copy in copies:
            copy.start()
        return copies

    handed = {2: hand_over(2)}

    for a in range(4):
        for load in loads[a]:
            load.wait()
        for b in range(blocks):
            def put_slab(r, carry):
                value = jnp.concatenate([
                    waves.at[a, b, h].reshape(WAVES * STEPS, HALF)[pl.ds(r, WAVES, stride=STEPS), :] for h in range(2)
                ], 1)
                slabs[a, b * STEPS + r] = stacked(value)
                return carry

            lax.fori_loop(0, STEPS, put_slab, 0)

    def own_products(r, total):
        a = 2 - 2 * own
        total = total + dot_rows(stacked(steps_p[0, STEPS + r]), slabs[a, r])
        return total - dot_rows(stacked(steps_p[1, STEPS + r]), slabs[a + 1, r])

    def other_products(r, total):
        a = 2 * own
        total = total + dot_rows(stacked(steps_other[0, r]), slabs[a, r])
        return total - dot_rows(stacked(steps_other[1, r]), slabs[a + 1, r])

    zero = jnp.zeros((2 * RANK, HALF), F32)
    mine = lax.fori_loop(*spans[2], own_products, zero, unroll=4)
    for copy in handed[2]:
        copy.wait_recv()
    theirs = lax.fori_loop(*spans[2], other_products, zero, unroll=4)

    for side, row0 in enumerate((0, STEPS + ROWS)):
        @pl.when(inside[side])
        def _():
            for copy in edges[side]:
                copy.wait_recv()
        put_speed(jnp.where(inside[side], speed_edges[side], 0.0), row0)
        for r in range(STEPS):
            steps_p[0, row0 + r] = jnp.where(inside[side], rows_of(probe_edges, side, r), 0.0)
    edge_sweeps(steps_p, speed, middle, beside, True)
    for index in range(2):
        handed[index] = hand_over(index)
    for index in range(2):
        mine = lax.fori_loop(*spans[index], own_products, mine, unroll=4)
    for index in range(2):
        for copy in handed[index]:
            copy.wait_recv()
        theirs = lax.fori_loop(*spans[index], other_products, theirs, unroll=4)

    def start(src, dst, k, device):
        copy = remote(src, dst, sum_send.at[k], sum_recv.at[k], device)
        copy.start()
        return copy

    def strip_sum(value):
        plane_send[...] = value
        copies = {d: start(plane_send, plane_recv.at[d - 1], d - 1, {"strip": plane_peer(d)}) for d in FAR_FIRST}
        for d in range(1, PLANE):
            copies[d].wait_recv()
            value = value + plane_recv[d - 1]
        column_send[...] = value
        more = {
            d: start(column_send, column_recv.at[d - 1], PLANE + d - 2, {"strip": column_peer(d)}) for d in COLUMN_FIRST
        }
        for d in range(1, SIDE):
            more[d].wait_recv()
            value = value + column_recv[d - 1]
        for copy in list(copies.values()) + list(more.values()):
            copy.wait_send()
        return value

    def gram_sum(value):
        first = PLANE + SIDE - 2
        gram_send[...] = value
        copies = {}
        for d in FAR_FIRST:
            copies[0, d] = start(gram_send, gram_recv.at[0, d], first + d, {"strip": plane_peer(d)})
            copies[1, d] = start(gram_send, gram_recv.at[1, d], first + PLANE + d, {"strip": plane_peer(d), "shot": away})
        copies[1, 0] = start(gram_send, gram_recv.at[1, 0], first + PLANE, {"shot": away})
        for d in range(1, PLANE):
            copies[0, d].wait_recv()
            value = value + gram_recv[0, d]
        copies[1, 0].wait_recv()
        other = gram_recv[1, 0]
        for d in range(1, PLANE):
            copies[1, d].wait_recv()
            other = other + gram_recv[1, d]
        pair = [value, other]
        for k in range(2):
            pair_send[k] = pair[k]
        more = {}
        for d in COLUMN_FIRST:
            more[d] = start(pair_send, pair_recv.at[d - 1], first + 2 * PLANE + d - 1, {"strip": column_peer(d)})
        for d in range(1, SIDE):
            more[d].wait_recv()
            pair = [pair[k] + pair_recv[d - 1, k] for k in range(2)]
        for copy in list(copies.values()) + list(more.values()):
            copy.wait_send()
        return pair

    folded = []
    for total in (mine, theirs):
        both = total[:RANK] + total[RANK:]
        folded.append(both + pltpu.roll(both, WAVES, 1))
    weight = strip_sum(jnp.where(lane < WAVES, folded[0], folded[1]))
    turned = pltpu.roll(weight, WAVES, 1)
    weights[0] = stacked(jnp.where(lane < WAVES, weight, turned))
    weights[1] = stacked(jnp.where(lane < WAVES, turned, weight))

    def combine(which, level, r):
        side = away if which else own
        both = dot(weights[which], slabs[2 * side + level, r])
        return both[:RANK] + both[RANK:]

    def for_other(level, r, carry):
        partial[level, r] = combine(1, level, r)
        return carry

    def for_own(level, r, carry):
        fields[level, STEPS + r] = combine(0, level, r)
        return carry

    def cross(level, index):
        lo, hi = spans[index]
        copy = remote(
            partial.at[level, pl.ds(lo, hi - lo)], arrived.at[level, pl.ds(lo, hi - lo)],
            core_send.at[2 * index + level], core_recv.at[2 * index + level], {"shot": away},
        )
        copy.start()
        return copy

    crossing = {}
    for level in range(2):
        for index in range(2):
            lax.fori_loop(*spans[index], functools.partial(for_other, level), 0, unroll=8)
            crossing[level, index] = cross(level, index)
    halos = {}
    for level in range(2):
        for index in range(2):
            lax.fori_loop(*spans[index], functools.partial(for_own, level), 0, unroll=8)
            crossing[level, index].wait_recv()
            lo, hi = spans[index]
            value = fields[level, STEPS + lo : STEPS + hi] + arrived[level, lo:hi]
            fields[level, STEPS + lo : STEPS + hi] = value
            leaving[index, level] = value
            target, landing = ((before, STEPS + ROWS), (after, 0))[index]
            at = level * index
            copy = remote(
                leaving.at[index, level, pl.ds(at, STEPS - level)],
                fields.at[level, pl.ds(landing + at, STEPS - level)],
                halo_send.at[index, level], halo_recv.at[index, level], {"strip": target},
            )
            halos[level, index] = copy
            pl.when(inside[index])(copy.start)
    for level in range(2):
        lax.fori_loop(*spans[2], functools.partial(for_other, level), 0, unroll=4)
        crossing[level, 2] = cross(level, 2)
    for level in range(2):
        lax.fori_loop(*spans[2], functools.partial(for_own, level), 0, unroll=4)
    for level in range(2):
        crossing[level, 2].wait_recv()
        lo, hi = spans[2]
        fields[level, STEPS + lo : STEPS + hi] = fields[level, STEPS + lo : STEPS + hi] + arrived[level, lo:hi]
    inner_sweeps(fields, speed, middle, beside, False)
    for side, row0 in enumerate((0, STEPS + ROWS)):
        @pl.when(inside[side])
        def _():
            for level in range(2):
                halos[level, 1 - side].wait_recv()

        @pl.when(jnp.logical_not(inside[side]))
        def _():
            for level in range(2):
                for r in range(STEPS):
                    fields[level, row0 + r] = jnp.zeros((RANK, COLS), F32)

    edge_sweeps(fields, speed, middle, beside, False)

    crossed = remote(
        fields.at[0, pl.ds(STEPS, ROWS)], sketches.at[own], core_send.at[6], core_recv.at[6], {"shot": away}
    )
    crossed.start()
    kept = pltpu.make_async_copy(fields.at[0, pl.ds(STEPS, ROWS)], sketches.at[own], keep_sem.at[0])
    kept.start()

    gram = jnp.zeros((2 * RANK, 2 * RANK), F32)
    for i in range(ROWS // 4):
        value = jnp.concatenate([stacked(fields[0, STEPS + 4 * i + j]) for j in range(4)], 1)
        gram = gram + dot_rows(value, value)
    gram = gram[:RANK] + gram[RANK:]
    gram = gram[:, :RANK] + gram[:, RANK:]
    packed = jnp.concatenate([gram[:8], gram[8:], jnp.zeros((8, HALF - 2 * RANK), F32)], 1)
    for side, packed in zip((own, away), gram_sum(packed)):
        gram = jnp.concatenate([packed, pltpu.roll(packed, HALF - RANK, 1)], 0)
        high, low = split(lower_inverse(gram) * scale)
        inverses[side, 0] = high
        inverses[side, 1] = low
    crossed.wait_recv()
    kept.wait()
    for side, out in enumerate((left_out, right_out)):
        high, low = (inverses[side, k][:, RANK : 2 * RANK] for k in range(2))
        lhs = jnp.concatenate([jnp.concatenate([high, high], 1), jnp.concatenate([low, low], 1)], 0)

        def put_block(b, carry):
            for r in range(STEPS):
                both = dot(lhs, stacked(sketches[side, b * STEPS + r]))
                value = both[:RANK] + both[RANK:]
                for h in range(2):
                    out.at[b, h].reshape(RANK * STEPS, HALF)[pl.ds(r, RANK, stride=STEPS), :] = (
                        value[:, h * HALF : (h + 1) * HALF]
                    )
            return carry

        lax.fori_loop(0, blocks, put_block, 0)

    crossed.wait_send()
    for side in range(2):
        @pl.when(inside[side])
        def _():
            for copy in edges[1 - side]:
                copy.wait_send()
            for level in range(2):
                halos[level, side].wait_send()

    for copy in crossing.values():
        copy.wait_send()
    for copies in handed.values():
        for copy in copies:
            copy.wait_send()


def shards(source_now, source_prev, adjoint_now, adjoint_prev, courant, probe_left, probe_right):
    waves = [a.reshape(WAVES, ROWS, COLS) for a in (source_now, source_prev, adjoint_now, adjoint_prev)]
    any_spec = pl.BlockSpec(memory_space=pl.ANY)
    vmem_spec = pl.BlockSpec(memory_space=pltpu.VMEM)
    dma = pltpu.SemaphoreType.DMA
    count = ROWS // STEPS
    scale = math.sqrt(ROWS * lax.axis_size("strip") * COLS)
    factors = pl.pallas_call(
        functools.partial(main_kernel, scale),
        out_shape=(pltpu.VMEM((count, 2, RANK, STEPS, HALF), F32),) * 2,
        in_specs=[any_spec] * 7,
        out_specs=(vmem_spec, vmem_spec),
        scratch_shapes=[
            pltpu.VMEM((4, count, 2, WAVES, STEPS, HALF), F32),
            pltpu.VMEM((4, ROWS, 2 * WAVES, COLS), BF16),
            pltpu.VMEM((count, 2, RANK, STEPS, HALF), F32),
            pltpu.VMEM((2, 2, RANK, STEPS, HALF), F32),
            pltpu.VMEM((ROWS, COLS), F32),
            pltpu.VMEM((2, STEPS, COLS), F32),
            pltpu.VMEM((TALL, 8, COLS), F32),
            pltpu.VMEM((TALL, 8, COLS), F32),
            pltpu.VMEM((COLS, COLS), BF16),
            pltpu.VMEM((2, TALL, RANK, COLS), F32),
            pltpu.VMEM((2, ROWS, RANK, COLS), F32),
            pltpu.VMEM((2, 2 * RANK, HALF), BF16),
            pltpu.VMEM((RANK, HALF), F32),
            pltpu.VMEM((PLANE - 1, RANK, HALF), F32),
            pltpu.VMEM((RANK, HALF), F32),
            pltpu.VMEM((SIDE - 1, RANK, HALF), F32),
            pltpu.VMEM((8, HALF), F32),
            pltpu.VMEM((2, PLANE, 8, HALF), F32),
            pltpu.VMEM((2, 8, HALF), F32),
            pltpu.VMEM((SIDE - 1, 2, 8, HALF), F32),
            pltpu.VMEM((2, ROWS, RANK, COLS), F32),
            pltpu.VMEM((2, 2, RANK, HALF), BF16),
            pltpu.VMEM((2, TALL, RANK, COLS), F32),
            pltpu.VMEM((2, 2, STEPS, RANK, COLS), F32),
            pltpu.VMEM((2, ROWS, RANK, COLS), F32),
            pltpu.VMEM((2, ROWS, RANK, COLS), F32),
            dma((1 + 2 * count + 8 * count,)),
            dma((2, 3)),
            dma((2, 3)),
            dma((3 * PLANE + 2 * SIDE - 3,)),
            dma((3 * PLANE + 2 * SIDE - 3,)),
            dma((8,)),
            dma((8,)),
            dma((2, 2)),
            dma((2, 2)),
            dma((3, 2)),
            dma((3, 2)),
            dma((1,)),
        ],
        compiler_params=pltpu.CompilerParams(
            collective_id=0, has_side_effects=True, vmem_limit_bytes=56 * 1024 * 1024
        ),
        name="sketch",
    )(*waves, courant, probe_left, probe_right)
    return tuple(factor.transpose(2, 0, 3, 1, 4).reshape(RANK, ROWS, COLS) for factor in factors)


def solution(mesh):
    return jax.shard_map(
        shards,
        mesh=mesh,
        in_specs=(P("shot", None, "strip", None),) * 4 + (P("strip", None),) + (P(None, "strip", None),) * 2,
        out_specs=(P(None, "strip", None), P(None, "strip", None)),
        check_vma=False,
    )
```

```python
import functools
import math

import jax
import jax.numpy as jnp
from jax import lax
from jax.experimental import pallas as pl
from jax.experimental.pallas import tpu as pltpu
from jax.sharding import PartitionSpec as P

STEPS = 8
WAVES = 64
RANK = 16
ROWS = 32
COLS = 256
HALF = 128
TALL = ROWS + 2 * STEPS
SIDE = 4
PLANE = SIDE * SIDE
MESH = pl.DeviceIdType.MESH


def hops(d):
    return sum(min(k, SIDE - k) for k in (d % SIDE, d // SIDE))


FAR_FIRST = sorted(range(1, PLANE), key=lambda d: -hops(d))
COLUMN_FIRST = (2, 1, 3)
F32 = jnp.float32
BF16 = jnp.bfloat16


def split(x):
    high = x.astype(BF16)
    low = (x - high.astype(F32)).astype(BF16)
    return high, low


def stacked(x):
    return jnp.concatenate(split(x), 0)


def dot_rows(a, b):
    return lax.dot_general(a, b, (((1,), (1,)), ((), ())), preferred_element_type=F32)


def dot(a, b):
    return lax.dot_general(a, b, (((1,), (0,)), ((), ())), preferred_element_type=F32)


def spread_of(cells, beside):
    count = cells.shape[0]
    both = dot(jnp.concatenate(split(cells.reshape(count * RANK, COLS)), 0), beside[...])
    return (both[: count * RANK] + both[count * RANK :]).reshape(count, 2, 8, COLS)


def load_rows(ref, low, count):
    return ref[pl.ds(low, count)].reshape(count, 2, 8, COLS)


def advance(buf, speed, middle, beside, level, starts, count, transposed):
    now = buf.at[lax.rem(level + 1, 2)]
    new = buf.at[lax.rem(level, 2)]
    pieces = []
    for low in starts:
        cells = load_rows(now, low - 1, count + 2)
        if transposed:
            cells = cells * speed[pl.ds(low - 1, count + 2)][:, None]
        pieces.append(cells)
    inner = [cells[1:-1] for cells in pieces]
    side = spread_of(inner[0] if len(inner) == 1 else jnp.concatenate(inner, 0), beside)
    for k, low in enumerate(starts):
        total = pieces[k][:-2] + pieces[k][2:] + side[k * count : (k + 1) * count]
        if not transposed:
            total = total * speed[pl.ds(low, count)][:, None]
        centre = load_rows(now, low, count) if transposed else inner[k]
        value = middle[pl.ds(low, count)][:, None] * centre - load_rows(new, low, count) + total
        new[pl.ds(low, count)] = value.reshape(count, RANK, COLS)


def inner_sweeps(buf, speed, middle, beside, transposed):
    for level in range(1, STEPS + 1):
        advance(buf, speed, middle, beside, level, (STEPS + level,), ROWS - 2 * level, transposed)


def edge_sweeps(buf, speed, middle, beside, transposed):
    def body(level, carry):
        advance(buf, speed, middle, beside, level, (level, STEPS + ROWS - level), STEPS, transposed)
        return carry

    lax.fori_loop(1, STEPS + 1, body, 0)


def lower_inverse(gram):
    row = lax.broadcasted_iota(jnp.int32, (RANK, HALF), 0)
    lane = lax.broadcasted_iota(jnp.int32, (RANK, HALF), 1)
    work = jnp.where(lane < RANK, gram, jnp.where(lane == row + RANK, 1.0, 0.0))
    for k in range(RANK):
        pivot = work[k : k + 1, k : k + 1]
        root = lax.rsqrt(pivot)
        line = work[k : k + 1, :] * root
        column = jnp.where(row[:, :1] > k, work[:, k : k + 1] * root, 0.0)
        work = jnp.where(row == k, line, work - column * line)
    return work


def main_kernel(
    scale, src_now, src_prev, adj_now, adj_prev, courant, probe_left, probe_right,
    left_out, right_out,
    waves, slabs, probes, probe_edges, speed_own, speed_edges, speed, middle, beside,
    steps_p, steps_other, weights, plane_send, plane_recv, column_send, column_recv, gram_send, gram_recv, pair_send, pair_recv, sketches, inverses,
    fields, leaving, partial, arrived,
    load_sem, edge_send, edge_recv, sum_send, sum_recv, core_send, core_recv, halo_send, halo_recv,
    step_send, step_recv, keep_sem,
):
    own = lax.axis_index("shot")
    away = 1 - own
    me = lax.axis_index("strip")
    count = lax.axis_size("strip")
    x, y, z = me % SIDE, (me // SIDE) % SIDE, me // PLANE
    after, before = (me + 1) % count, (me + count - 1) % count
    lane = lax.broadcasted_iota(jnp.int32, (RANK, HALF), 1)
    blocks = ROWS // STEPS
    targets = ((after, ROWS - STEPS), (before, 0))
    halves = [pl.ds(0, HALF), pl.ds(HALF, HALF)]

    def plane_peer(d):
        return z * PLANE + ((y + d // SIDE) % SIDE) * SIDE + (x + d % SIDE) % SIDE

    def column_peer(d):
        return ((z + d) % SIDE) * PLANE + y * SIDE + x

    def remote(src, dst, send, recv, device):
        return pltpu.make_async_remote_copy(
            src_ref=src, dst_ref=dst, send_sem=send, recv_sem=recv, device_id=device, device_id_type=MESH
        )

    barrier = pltpu.get_barrier_semaphore()
    inside = (me > 0, me < count - 1)
    for side, peer in enumerate((before, after)):
        @pl.when(inside[side])
        def _():
            pl.semaphore_signal(barrier, inc=1, device_id={"strip": peer}, device_id_type=MESH)
    strips = [plane_peer(d) for d in FAR_FIRST] + [column_peer(d) for d in COLUMN_FIRST]
    for peer in strips:
        pl.semaphore_signal(barrier, inc=1, device_id={"strip": peer}, device_id_type=MESH)
    pl.semaphore_signal(barrier, inc=1, device_id={"shot": away}, device_id_type=MESH)
    for d in FAR_FIRST:
        pl.semaphore_signal(barrier, inc=1, device_id={"strip": plane_peer(d), "shot": away}, device_id_type=MESH)

    def probe_loads(probe):
        return [
            pltpu.make_async_copy(probe.at[:, pl.ds(b * STEPS, STEPS), halves[h]], probes.at[b, h], load_sem.at[1 + 2 * b + h])
            for b in range(blocks)
            for h in range(2)
        ]

    def edge_copies(side):
        target, first = targets[side]
        speed_copy = remote(speed_own.at[pl.ds(first, STEPS)], speed_edges.at[side],
                            edge_send.at[side, 0], edge_recv.at[side, 0], {"strip": target})
        return [speed_copy] + [
            remote(probes.at[first // STEPS, h], probe_edges.at[side, h],
                   edge_send.at[side, 1 + h], edge_recv.at[side, 1 + h], {"strip": target})
            for h in range(2)
        ]

    load_speed = pltpu.make_async_copy(courant, speed_own, load_sem.at[0])
    load_speed.start()
    for core, probe in enumerate((probe_left, probe_right)):
        @pl.when(own == core)
        def _():
            for load in probe_loads(probe):
                load.start()
    base = 1 + 2 * blocks
    loads = [
        [
            pltpu.make_async_copy(
                wave.at[:, pl.ds(b * STEPS, STEPS), halves[h]], waves.at[a, b, h],
                load_sem.at[base + (a * blocks + b) * 2 + h],
            )
            for b in range(blocks)
            for h in range(2)
        ]
        for a, wave in enumerate((src_now, src_prev, adj_now, adj_prev))
    ]
    for group in loads:
        for load in group:
            load.start()

    load_speed.wait()
    for load in probe_loads(probe_left):
        load.wait()
    pl.semaphore_wait(barrier, len(strips) + PLANE + sum(flag.astype(jnp.int32) for flag in inside))

    edges = [edge_copies(side) for side in range(2)]
    for side in range(2):
        @pl.when(inside[1 - side])
        def _():
            for copy in edges[side]:
                copy.start()

    near = lax.broadcasted_iota(jnp.int32, (COLS, COLS), 0) - lax.broadcasted_iota(jnp.int32, (COLS, COLS), 1)
    beside[...] = jnp.where(jnp.abs(near) == 1, 1.0, 0.0).astype(BF16)

    def put_speed(values, row0):
        for r in range(STEPS):
            value = jnp.broadcast_to(values[r : r + 1, :], (8, COLS))
            speed[row0 + r] = value
            middle[row0 + r] = 2.0 - 4.0 * value

    for block in range(blocks):
        put_speed(speed_own[pl.ds(block * STEPS, STEPS), :], STEPS + block * STEPS)
    def rows_of(tiles, b, r):
        return jnp.concatenate([
            tiles.at[b, h].reshape(RANK * STEPS, HALF)[pl.ds(r, RANK, stride=STEPS), :] for h in range(2)
        ], 1)

    for b in range(blocks):
        for r in range(STEPS):
            steps_p[0, STEPS + b * STEPS + r] = rows_of(probes, b, r)

    def put_zero(r, carry):
        steps_p[1, r] = jnp.zeros((RANK, COLS), F32)
        return carry

    lax.fori_loop(0, TALL, put_zero, 0)

    inner_sweeps(steps_p, speed, middle, beside, True)

    spans = ((0, STEPS), (ROWS - STEPS, ROWS), (STEPS, ROWS - STEPS))

    def hand_over(index):
        lo, hi = spans[index]
        copies = [
            remote(steps_p.at[level, pl.ds(STEPS + lo, hi - lo)], steps_other.at[level, pl.ds(lo, hi - lo)],
                   step_send.at[index, level], step_recv.at[index, level], {"shot": away})
            for level in range(2)
        ]
        for copy in copies:
            copy.start()
        return copies

    handed = {2: hand_over(2)}

    for a in range(4):
        for load in loads[a]:
            load.wait()
        for b in range(blocks):
            def put_slab(r, carry):
                value = jnp.concatenate([
                    waves.at[a, b, h].reshape(WAVES * STEPS, HALF)[pl.ds(r, WAVES, stride=STEPS), :] for h in range(2)
                ], 1)
                slabs[a, b * STEPS + r] = stacked(value)
                return carry

            lax.fori_loop(0, STEPS, put_slab, 0)

    def own_products(r, total):
        a = 2 - 2 * own
        total = total + dot_rows(stacked(steps_p[0, STEPS + r]), slabs[a, r])
        return total - dot_rows(stacked(steps_p[1, STEPS + r]), slabs[a + 1, r])

    def other_products(r, total):
        a = 2 * own
        total = total + dot_rows(stacked(steps_other[0, r]), slabs[a, r])
        return total - dot_rows(stacked(steps_other[1, r]), slabs[a + 1, r])

    zero = jnp.zeros((2 * RANK, HALF), F32)
    mine = lax.fori_loop(*spans[2], own_products, zero, unroll=4)
    for copy in handed[2]:
        copy.wait_recv()
    theirs = lax.fori_loop(*spans[2], other_products, zero, unroll=4)

    for side, row0 in enumerate((0, STEPS + ROWS)):
        @pl.when(inside[side])
        def _():
            for copy in edges[side]:
                copy.wait_recv()
        put_speed(jnp.where(inside[side], speed_edges[side], 0.0), row0)
        for r in range(STEPS):
            steps_p[0, row0 + r] = jnp.where(inside[side], rows_of(probe_edges, side, r), 0.0)
    edge_sweeps(steps_p, speed, middle, beside, True)
    for index in range(2):
        handed[index] = hand_over(index)
    edge_rows = [r for index in range(2) for r in range(*spans[index])]
    for r in edge_rows:
        mine = own_products(r, mine)
    for index in range(2):
        for copy in handed[index]:
            copy.wait_recv()
    for r in edge_rows:
        theirs = other_products(r, theirs)

    def start(src, dst, k, device):
        copy = remote(src, dst, sum_send.at[k], sum_recv.at[k], device)
        copy.start()
        return copy

    def strip_sum(value):
        plane_send[...] = value
        copies = {d: start(plane_send, plane_recv.at[d - 1], d - 1, {"strip": plane_peer(d)}) for d in FAR_FIRST}
        for d in range(1, PLANE):
            copies[d].wait_recv()
            value = value + plane_recv[d - 1]
        column_send[...] = value
        more = {
            d: start(column_send, column_recv.at[d - 1], PLANE + d - 2, {"strip": column_peer(d)}) for d in COLUMN_FIRST
        }
        for d in range(1, SIDE):
            more[d].wait_recv()
            value = value + column_recv[d - 1]
        for copy in list(copies.values()) + list(more.values()):
            copy.wait_send()
        return value

    def gram_sum(value):
        first = PLANE + SIDE - 2
        gram_send[...] = value
        copies = {}
        for d in FAR_FIRST:
            copies[0, d] = start(gram_send, gram_recv.at[0, d], first + d, {"strip": plane_peer(d)})
            copies[1, d] = start(gram_send, gram_recv.at[1, d], first + PLANE + d, {"strip": plane_peer(d), "shot": away})
        copies[1, 0] = start(gram_send, gram_recv.at[1, 0], first + PLANE, {"shot": away})
        for d in range(1, PLANE):
            copies[0, d].wait_recv()
            value = value + gram_recv[0, d]
        copies[1, 0].wait_recv()
        other = gram_recv[1, 0]
        for d in range(1, PLANE):
            copies[1, d].wait_recv()
            other = other + gram_recv[1, d]
        pair = [value, other]
        for k in range(2):
            pair_send[k] = pair[k]
        more = {}
        for d in COLUMN_FIRST:
            more[d] = start(pair_send, pair_recv.at[d - 1], first + 2 * PLANE + d - 1, {"strip": column_peer(d)})
        for d in range(1, SIDE):
            more[d].wait_recv()
            pair = [pair[k] + pair_recv[d - 1, k] for k in range(2)]
        for copy in list(copies.values()) + list(more.values()):
            copy.wait_send()
        return pair

    folded = []
    for total in (mine, theirs):
        both = total[:RANK] + total[RANK:]
        folded.append(both + pltpu.roll(both, WAVES, 1))
    weight = strip_sum(jnp.where(lane < WAVES, folded[0], folded[1]))
    turned = pltpu.roll(weight, WAVES, 1)
    weights[0] = stacked(jnp.where(lane < WAVES, weight, turned))
    weights[1] = stacked(jnp.where(lane < WAVES, turned, weight))

    def combine(which, level, r):
        side = away if which else own
        both = dot(weights[which], slabs[2 * side + level, r])
        return both[:RANK] + both[RANK:]

    def for_other(level, r, carry):
        partial[level, r] = combine(1, level, r)
        return carry

    def for_own(level, r, carry):
        fields[level, STEPS + r] = combine(0, level, r)
        return carry

    def cross(level, index):
        lo, hi = spans[index]
        copy = remote(
            partial.at[level, pl.ds(lo, hi - lo)], arrived.at[level, pl.ds(lo, hi - lo)],
            core_send.at[2 * index + level], core_recv.at[2 * index + level], {"shot": away},
        )
        copy.start()
        return copy

    crossing = {}
    for level in range(2):
        for r in edge_rows:
            for_other(level, r, 0)
        for index in range(2):
            crossing[level, index] = cross(level, index)
    halos = {}
    for level in range(2):
        for r in edge_rows:
            for_own(level, r, 0)
        for index in range(2):
            crossing[level, index].wait_recv()
            lo, hi = spans[index]
            value = fields[level, STEPS + lo : STEPS + hi] + arrived[level, lo:hi]
            fields[level, STEPS + lo : STEPS + hi] = value
            leaving[index, level] = value
            target, landing = ((before, STEPS + ROWS), (after, 0))[index]
            at = level * index
            copy = remote(
                leaving.at[index, level, pl.ds(at, STEPS - level)],
                fields.at[level, pl.ds(landing + at, STEPS - level)],
                halo_send.at[index, level], halo_recv.at[index, level], {"strip": target},
            )
            halos[level, index] = copy
            pl.when(inside[index])(copy.start)
    for level in range(2):
        lax.fori_loop(*spans[2], functools.partial(for_other, level), 0, unroll=4)
        crossing[level, 2] = cross(level, 2)
    for level in range(2):
        lax.fori_loop(*spans[2], functools.partial(for_own, level), 0, unroll=4)
    for level in range(2):
        crossing[level, 2].wait_recv()
        lo, hi = spans[2]
        fields[level, STEPS + lo : STEPS + hi] = fields[level, STEPS + lo : STEPS + hi] + arrived[level, lo:hi]
    inner_sweeps(fields, speed, middle, beside, False)

    def gram_of(i):
        value = jnp.concatenate([stacked(fields[0, STEPS + 4 * i + j]) for j in range(4)], 1)
        return dot_rows(value, value)

    gram = jnp.zeros((2 * RANK, 2 * RANK), F32)
    for i in range(STEPS // 4, (ROWS - STEPS) // 4):
        gram = gram + gram_of(i)
    for side, row0 in enumerate((0, STEPS + ROWS)):
        @pl.when(inside[side])
        def _():
            for level in range(2):
                halos[level, 1 - side].wait_recv()

        @pl.when(jnp.logical_not(inside[side]))
        def _():
            for level in range(2):
                for r in range(STEPS):
                    fields[level, row0 + r] = jnp.zeros((RANK, COLS), F32)

    edge_sweeps(fields, speed, middle, beside, False)

    crossed = remote(
        fields.at[0, pl.ds(STEPS, ROWS)], sketches.at[own], core_send.at[6], core_recv.at[6], {"shot": away}
    )
    crossed.start()
    kept = pltpu.make_async_copy(fields.at[0, pl.ds(STEPS, ROWS)], sketches.at[own], keep_sem.at[0])
    kept.start()

    for i in list(range(STEPS // 4)) + list(range((ROWS - STEPS) // 4, ROWS // 4)):
        gram = gram + gram_of(i)
    gram = gram[:RANK] + gram[RANK:]
    gram = gram[:, :RANK] + gram[:, RANK:]
    packed = jnp.concatenate([gram[:8], gram[8:], jnp.zeros((8, HALF - 2 * RANK), F32)], 1)
    for side, packed in zip((own, away), gram_sum(packed)):
        gram = jnp.concatenate([packed, pltpu.roll(packed, HALF - RANK, 1)], 0)
        high, low = split(lower_inverse(gram) * scale)
        inverses[side, 0] = high
        inverses[side, 1] = low
    crossed.wait_recv()
    kept.wait()
    for side, out in enumerate((left_out, right_out)):
        high, low = (inverses[side, k][:, RANK : 2 * RANK] for k in range(2))
        lhs = jnp.concatenate([jnp.concatenate([high, high], 1), jnp.concatenate([low, low], 1)], 0)

        def put_block(b, carry):
            for r in range(STEPS):
                both = dot(lhs, stacked(sketches[side, b * STEPS + r]))
                value = both[:RANK] + both[RANK:]
                for h in range(2):
                    out.at[b, h].reshape(RANK * STEPS, HALF)[pl.ds(r, RANK, stride=STEPS), :] = (
                        value[:, h * HALF : (h + 1) * HALF]
                    )
            return carry

        lax.fori_loop(0, blocks, put_block, 0, unroll=blocks)

    crossed.wait_send()
    for side in range(2):
        @pl.when(inside[side])
        def _():
            for copy in edges[1 - side]:
                copy.wait_send()
            for level in range(2):
                halos[level, side].wait_send()

    for copy in crossing.values():
        copy.wait_send()
    for copies in handed.values():
        for copy in copies:
            copy.wait_send()


def shards(source_now, source_prev, adjoint_now, adjoint_prev, courant, probe_left, probe_right):
    waves = [a.reshape(WAVES, ROWS, COLS) for a in (source_now, source_prev, adjoint_now, adjoint_prev)]
    any_spec = pl.BlockSpec(memory_space=pl.ANY)
    vmem_spec = pl.BlockSpec(memory_space=pltpu.VMEM)
    dma = pltpu.SemaphoreType.DMA
    count = ROWS // STEPS
    scale = math.sqrt(ROWS * lax.axis_size("strip") * COLS)
    factors = pl.pallas_call(
        functools.partial(main_kernel, scale),
        out_shape=(pltpu.VMEM((count, 2, RANK, STEPS, HALF), F32),) * 2,
        in_specs=[any_spec] * 7,
        out_specs=(vmem_spec, vmem_spec),
        scratch_shapes=[
            pltpu.VMEM((4, count, 2, WAVES, STEPS, HALF), F32),
            pltpu.VMEM((4, ROWS, 2 * WAVES, COLS), BF16),
            pltpu.VMEM((count, 2, RANK, STEPS, HALF), F32),
            pltpu.VMEM((2, 2, RANK, STEPS, HALF), F32),
            pltpu.VMEM((ROWS, COLS), F32),
            pltpu.VMEM((2, STEPS, COLS), F32),
            pltpu.VMEM((TALL, 8, COLS), F32),
            pltpu.VMEM((TALL, 8, COLS), F32),
            pltpu.VMEM((COLS, COLS), BF16),
            pltpu.VMEM((2, TALL, RANK, COLS), F32),
            pltpu.VMEM((2, ROWS, RANK, COLS), F32),
            pltpu.VMEM((2, 2 * RANK, HALF), BF16),
            pltpu.VMEM((RANK, HALF), F32),
            pltpu.VMEM((PLANE - 1, RANK, HALF), F32),
            pltpu.VMEM((RANK, HALF), F32),
            pltpu.VMEM((SIDE - 1, RANK, HALF), F32),
            pltpu.VMEM((8, HALF), F32),
            pltpu.VMEM((2, PLANE, 8, HALF), F32),
            pltpu.VMEM((2, 8, HALF), F32),
            pltpu.VMEM((SIDE - 1, 2, 8, HALF), F32),
            pltpu.VMEM((2, ROWS, RANK, COLS), F32),
            pltpu.VMEM((2, 2, RANK, HALF), BF16),
            pltpu.VMEM((2, TALL, RANK, COLS), F32),
            pltpu.VMEM((2, 2, STEPS, RANK, COLS), F32),
            pltpu.VMEM((2, ROWS, RANK, COLS), F32),
            pltpu.VMEM((2, ROWS, RANK, COLS), F32),
            dma((1 + 2 * count + 8 * count,)),
            dma((2, 3)),
            dma((2, 3)),
            dma((3 * PLANE + 2 * SIDE - 3,)),
            dma((3 * PLANE + 2 * SIDE - 3,)),
            dma((8,)),
            dma((8,)),
            dma((2, 2)),
            dma((2, 2)),
            dma((3, 2)),
            dma((3, 2)),
            dma((1,)),
        ],
        compiler_params=pltpu.CompilerParams(
            collective_id=0, has_side_effects=True, vmem_limit_bytes=56 * 1024 * 1024
        ),
        name="sketch",
    )(*waves, courant, probe_left, probe_right)
    return tuple(factor.transpose(2, 0, 3, 1, 4).reshape(RANK, ROWS, COLS) for factor in factors)


def solution(mesh):
    return jax.shard_map(
        shards,
        mesh=mesh,
        in_specs=(P("shot", None, "strip", None),) * 4 + (P("strip", None),) + (P(None, "strip", None),) * 2,
        out_specs=(P(None, "strip", None), P(None, "strip", None)),
        check_vma=False,
    )
```

```python
import functools
import math

import jax
import jax.numpy as jnp
from jax import lax
from jax.experimental import pallas as pl
from jax.experimental.pallas import tpu as pltpu
from jax.sharding import PartitionSpec as P

STEPS = 8
WAVES = 64
RANK = 16
ROWS = 32
COLS = 256
HALF = 128
TALL = ROWS + 2 * STEPS
SIDE = 4
PLANE = SIDE * SIDE
MESH = pl.DeviceIdType.MESH


def hops(d):
    return sum(min(k, SIDE - k) for k in (d % SIDE, d // SIDE))


FAR_FIRST = sorted(range(1, PLANE), key=lambda d: -hops(d))
COLUMN_FIRST = (2, 1, 3)
F32 = jnp.float32
BF16 = jnp.bfloat16


def split(x):
    high = x.astype(BF16)
    low = (x - high.astype(F32)).astype(BF16)
    return high, low


def stacked(x):
    return jnp.concatenate(split(x), 0)


def dot_rows(a, b):
    return lax.dot_general(a, b, (((1,), (1,)), ((), ())), preferred_element_type=F32)


def dot(a, b):
    return lax.dot_general(a, b, (((1,), (0,)), ((), ())), preferred_element_type=F32)


def spread_of(cells, beside):
    count = cells.shape[0]
    both = dot(jnp.concatenate(split(cells.reshape(count * RANK, COLS)), 0), beside[...])
    return (both[: count * RANK] + both[count * RANK :]).reshape(count, 2, 8, COLS)


def load_rows(ref, low, count):
    return ref[pl.ds(low, count)].reshape(count, 2, 8, COLS)


def advance(buf, speed, middle, beside, level, starts, count, transposed):
    now, new = buf.at[(level + 1) % 2], buf.at[level % 2]
    pieces = []
    for low in starts:
        cells = load_rows(now, low - 1, count + 2)
        if transposed:
            cells = cells * speed[pl.ds(low - 1, count + 2)][:, None]
        pieces.append(cells)
    inner = [cells[1:-1] for cells in pieces]
    side = spread_of(inner[0] if len(inner) == 1 else jnp.concatenate(inner, 0), beside)
    for k, low in enumerate(starts):
        total = pieces[k][:-2] + pieces[k][2:] + side[k * count : (k + 1) * count]
        if not transposed:
            total = total * speed[pl.ds(low, count)][:, None]
        centre = load_rows(now, low, count) if transposed else inner[k]
        value = middle[pl.ds(low, count)][:, None] * centre - load_rows(new, low, count) + total
        new[pl.ds(low, count)] = value.reshape(count, RANK, COLS)


def inner_sweeps(buf, speed, middle, beside, transposed):
    for level in range(1, STEPS + 1):
        advance(buf, speed, middle, beside, level, (STEPS + level,), ROWS - 2 * level, transposed)


def edge_sweeps(buf, speed, middle, beside, transposed):
    def body(level, carry):
        advance(buf, speed, middle, beside, level, (level, STEPS + ROWS - level), STEPS, transposed)
        return carry

    for level in range(1, STEPS + 1):
        body(level, 0)


def lower_inverse(gram):
    row = lax.broadcasted_iota(jnp.int32, (RANK, HALF), 0)
    lane = lax.broadcasted_iota(jnp.int32, (RANK, HALF), 1)
    work = jnp.where(lane < RANK, gram, jnp.where(lane == row + RANK, 1.0, 0.0))
    for k in range(RANK):
        pivot = work[k : k + 1, k : k + 1]
        root = lax.rsqrt(pivot)
        line = work[k : k + 1, :] * root
        column = jnp.where(row[:, :1] > k, work[:, k : k + 1] * root, 0.0)
        work = jnp.where(row == k, line, work - column * line)
    return work


def main_kernel(
    scale, src_now, src_prev, adj_now, adj_prev, courant, probe_left, probe_right,
    left_out, right_out,
    waves, slabs, probes, probe_edges, speed_own, speed_edges, speed, middle, beside,
    steps_p, steps_other, weights, plane_send, plane_recv, column_send, column_recv, gram_send, gram_recv, pair_send, pair_recv, sketches, inverses,
    fields, leaving, partial, arrived,
    load_sem, edge_send, edge_recv, sum_send, sum_recv, core_send, core_recv, halo_send, halo_recv,
    step_send, step_recv, keep_sem,
):
    own = lax.axis_index("shot")
    away = 1 - own
    me = lax.axis_index("strip")
    count = lax.axis_size("strip")
    x, y, z = me % SIDE, (me // SIDE) % SIDE, me // PLANE
    after, before = (me + 1) % count, (me + count - 1) % count
    lane = lax.broadcasted_iota(jnp.int32, (RANK, HALF), 1)
    blocks = ROWS // STEPS
    targets = ((after, ROWS - STEPS), (before, 0))
    halves = [pl.ds(0, HALF), pl.ds(HALF, HALF)]

    def plane_peer(d):
        return z * PLANE + ((y + d // SIDE) % SIDE) * SIDE + (x + d % SIDE) % SIDE

    def column_peer(d):
        return ((z + d) % SIDE) * PLANE + y * SIDE + x

    def remote(src, dst, send, recv, device):
        return pltpu.make_async_remote_copy(
            src_ref=src, dst_ref=dst, send_sem=send, recv_sem=recv, device_id=device, device_id_type=MESH
        )

    barrier = pltpu.get_barrier_semaphore()
    inside = (me > 0, me < count - 1)
    for side, peer in enumerate((before, after)):
        @pl.when(inside[side])
        def _():
            pl.semaphore_signal(barrier, inc=1, device_id={"strip": peer}, device_id_type=MESH)
    strips = [plane_peer(d) for d in FAR_FIRST] + [column_peer(d) for d in COLUMN_FIRST]
    for peer in strips:
        pl.semaphore_signal(barrier, inc=1, device_id={"strip": peer}, device_id_type=MESH)
    pl.semaphore_signal(barrier, inc=1, device_id={"shot": away}, device_id_type=MESH)
    for d in FAR_FIRST:
        pl.semaphore_signal(barrier, inc=1, device_id={"strip": plane_peer(d), "shot": away}, device_id_type=MESH)

    def probe_loads(probe):
        return [
            pltpu.make_async_copy(probe.at[:, pl.ds(b * STEPS, STEPS), halves[h]], probes.at[b, h], load_sem.at[1 + 2 * b + h])
            for b in range(blocks)
            for h in range(2)
        ]

    def edge_copies(side):
        target, first = targets[side]
        speed_copy = remote(speed_own.at[pl.ds(first, STEPS)], speed_edges.at[side],
                            edge_send.at[side, 0], edge_recv.at[side, 0], {"strip": target})
        return [speed_copy] + [
            remote(probes.at[first // STEPS, h], probe_edges.at[side, h],
                   edge_send.at[side, 1 + h], edge_recv.at[side, 1 + h], {"strip": target})
            for h in range(2)
        ]

    load_speed = pltpu.make_async_copy(courant, speed_own, load_sem.at[0])
    load_speed.start()
    for core, probe in enumerate((probe_left, probe_right)):
        @pl.when(own == core)
        def _():
            for load in probe_loads(probe):
                load.start()
    base = 1 + 2 * blocks
    loads = [
        [
            pltpu.make_async_copy(
                wave.at[:, pl.ds(b * STEPS, STEPS), halves[h]], waves.at[a, b, h],
                load_sem.at[base + (a * blocks + b) * 2 + h],
            )
            for b in range(blocks)
            for h in range(2)
        ]
        for a, wave in enumerate((src_now, src_prev, adj_now, adj_prev))
    ]
    for group in loads:
        for load in group:
            load.start()

    load_speed.wait()
    for load in probe_loads(probe_left):
        load.wait()
    pl.semaphore_wait(barrier, len(strips) + PLANE + sum(flag.astype(jnp.int32) for flag in inside))

    edges = [edge_copies(side) for side in range(2)]
    for side in range(2):
        @pl.when(inside[1 - side])
        def _():
            for copy in edges[side]:
                copy.start()

    near = lax.broadcasted_iota(jnp.int32, (COLS, COLS), 0) - lax.broadcasted_iota(jnp.int32, (COLS, COLS), 1)
    beside[...] = jnp.where(jnp.abs(near) == 1, 1.0, 0.0).astype(BF16)

    def put_speed(values, row0):
        for r in range(STEPS):
            value = jnp.broadcast_to(values[r : r + 1, :], (8, COLS))
            speed[row0 + r] = value
            middle[row0 + r] = 2.0 - 4.0 * value

    for block in range(blocks):
        put_speed(speed_own[pl.ds(block * STEPS, STEPS), :], STEPS + block * STEPS)
    def rows_of(tiles, b, r):
        return jnp.concatenate([
            tiles.at[b, h].reshape(RANK * STEPS, HALF)[pl.ds(r, RANK, stride=STEPS), :] for h in range(2)
        ], 1)

    for b in range(blocks):
        for r in range(STEPS):
            steps_p[0, STEPS + b * STEPS + r] = rows_of(probes, b, r)

    def put_zero(r, carry):
        steps_p[1, r] = jnp.zeros((RANK, COLS), F32)
        return carry

    lax.fori_loop(0, TALL, put_zero, 0)

    inner_sweeps(steps_p, speed, middle, beside, True)

    spans = ((0, STEPS), (ROWS - STEPS, ROWS), (STEPS, ROWS - STEPS))

    def hand_over(index):
        lo, hi = spans[index]
        copies = [
            remote(steps_p.at[level, pl.ds(STEPS + lo, hi - lo)], steps_other.at[level, pl.ds(lo, hi - lo)],
                   step_send.at[index, level], step_recv.at[index, level], {"shot": away})
            for level in range(2)
        ]
        for copy in copies:
            copy.start()
        return copies

    handed = {2: hand_over(2)}

    for a in range(4):
        for load in loads[a]:
            load.wait()
        for b in range(blocks):
            def put_slab(r, carry):
                value = jnp.concatenate([
                    waves.at[a, b, h].reshape(WAVES * STEPS, HALF)[pl.ds(r, WAVES, stride=STEPS), :] for h in range(2)
                ], 1)
                slabs[a, b * STEPS + r] = stacked(value)
                return carry

            lax.fori_loop(0, STEPS, put_slab, 0)

    def own_products(r, total):
        a = 2 - 2 * own
        total = total + dot_rows(stacked(steps_p[0, STEPS + r]), slabs[a, r])
        return total - dot_rows(stacked(steps_p[1, STEPS + r]), slabs[a + 1, r])

    def other_products(r, total):
        a = 2 * own
        total = total + dot_rows(stacked(steps_other[0, r]), slabs[a, r])
        return total - dot_rows(stacked(steps_other[1, r]), slabs[a + 1, r])

    zero = jnp.zeros((2 * RANK, HALF), F32)
    mine = lax.fori_loop(*spans[2], own_products, zero, unroll=4)
    for copy in handed[2]:
        copy.wait_recv()
    theirs = lax.fori_loop(*spans[2], other_products, zero, unroll=4)

    for side, row0 in enumerate((0, STEPS + ROWS)):
        @pl.when(inside[side])
        def _():
            for copy in edges[side]:
                copy.wait_recv()
        put_speed(jnp.where(inside[side], speed_edges[side], 0.0), row0)
        for r in range(STEPS):
            steps_p[0, row0 + r] = jnp.where(inside[side], rows_of(probe_edges, side, r), 0.0)
    edge_sweeps(steps_p, speed, middle, beside, True)
    for index in range(2):
        handed[index] = hand_over(index)
    edge_rows = [r for index in range(2) for r in range(*spans[index])]
    for r in edge_rows:
        mine = own_products(r, mine)
    for index in range(2):
        for copy in handed[index]:
            copy.wait_recv()
    for r in edge_rows:
        theirs = other_products(r, theirs)

    def start(src, dst, k, device):
        copy = remote(src, dst, sum_send.at[k], sum_recv.at[k], device)
        copy.start()
        return copy

    def strip_sum(value):
        plane_send[...] = value
        copies = {d: start(plane_send, plane_recv.at[d - 1], d - 1, {"strip": plane_peer(d)}) for d in FAR_FIRST}
        for d in range(1, PLANE):
            copies[d].wait_recv()
            value = value + plane_recv[d - 1]
        column_send[...] = value
        more = {
            d: start(column_send, column_recv.at[d - 1], PLANE + d - 2, {"strip": column_peer(d)}) for d in COLUMN_FIRST
        }
        for d in range(1, SIDE):
            more[d].wait_recv()
            value = value + column_recv[d - 1]
        for copy in list(copies.values()) + list(more.values()):
            copy.wait_send()
        return value

    def gram_sum(value):
        first = PLANE + SIDE - 2
        gram_send[...] = value
        copies = {}
        for d in FAR_FIRST:
            copies[0, d] = start(gram_send, gram_recv.at[0, d], first + d, {"strip": plane_peer(d)})
            copies[1, d] = start(gram_send, gram_recv.at[1, d], first + PLANE + d, {"strip": plane_peer(d), "shot": away})
        copies[1, 0] = start(gram_send, gram_recv.at[1, 0], first + PLANE, {"shot": away})
        for d in range(1, PLANE):
            copies[0, d].wait_recv()
            value = value + gram_recv[0, d]
        copies[1, 0].wait_recv()
        other = gram_recv[1, 0]
        for d in range(1, PLANE):
            copies[1, d].wait_recv()
            other = other + gram_recv[1, d]
        pair = [value, other]
        for k in range(2):
            pair_send[k] = pair[k]
        more = {}
        for d in COLUMN_FIRST:
            more[d] = start(pair_send, pair_recv.at[d - 1], first + 2 * PLANE + d - 1, {"strip": column_peer(d)})
        for d in range(1, SIDE):
            more[d].wait_recv()
            pair = [pair[k] + pair_recv[d - 1, k] for k in range(2)]
        for copy in list(copies.values()) + list(more.values()):
            copy.wait_send()
        return pair

    folded = []
    for total in (mine, theirs):
        both = total[:RANK] + total[RANK:]
        folded.append(both + pltpu.roll(both, WAVES, 1))
    weight = strip_sum(jnp.where(lane < WAVES, folded[0], folded[1]))
    turned = pltpu.roll(weight, WAVES, 1)
    weights[0] = stacked(jnp.where(lane < WAVES, weight, turned))
    weights[1] = stacked(jnp.where(lane < WAVES, turned, weight))

    def combine(which, level, r):
        side = away if which else own
        both = dot(weights[which], slabs[2 * side + level, r])
        return both[:RANK] + both[RANK:]

    def for_other(level, r, carry):
        partial[level, r] = combine(1, level, r)
        return carry

    def for_own(level, r, carry):
        fields[level, STEPS + r] = combine(0, level, r)
        return carry

    def cross(level, index):
        lo, hi = spans[index]
        copy = remote(
            partial.at[level, pl.ds(lo, hi - lo)], arrived.at[level, pl.ds(lo, hi - lo)],
            core_send.at[2 * index + level], core_recv.at[2 * index + level], {"shot": away},
        )
        copy.start()
        return copy

    crossing = {}
    for level in range(2):
        for r in edge_rows:
            for_other(level, r, 0)
        for index in range(2):
            crossing[level, index] = cross(level, index)
    halos = {}
    for level in range(2):
        for r in edge_rows:
            for_own(level, r, 0)
        for index in range(2):
            crossing[level, index].wait_recv()
            lo, hi = spans[index]
            value = fields[level, STEPS + lo : STEPS + hi] + arrived[level, lo:hi]
            fields[level, STEPS + lo : STEPS + hi] = value
            leaving[index, level] = value
            target, landing = ((before, STEPS + ROWS), (after, 0))[index]
            at = level * index
            copy = remote(
                leaving.at[index, level, pl.ds(at, STEPS - level)],
                fields.at[level, pl.ds(landing + at, STEPS - level)],
                halo_send.at[index, level], halo_recv.at[index, level], {"strip": target},
            )
            halos[level, index] = copy
            pl.when(inside[index])(copy.start)
    for level in range(2):
        lax.fori_loop(*spans[2], functools.partial(for_other, level), 0, unroll=4)
        crossing[level, 2] = cross(level, 2)
    for level in range(2):
        lax.fori_loop(*spans[2], functools.partial(for_own, level), 0, unroll=4)
    for level in range(2):
        crossing[level, 2].wait_recv()
        lo, hi = spans[2]
        fields[level, STEPS + lo : STEPS + hi] = fields[level, STEPS + lo : STEPS + hi] + arrived[level, lo:hi]
    inner_sweeps(fields, speed, middle, beside, False)

    def gram_of(i):
        value = jnp.concatenate([stacked(fields[0, STEPS + 4 * i + j]) for j in range(4)], 1)
        return dot_rows(value, value)

    gram = jnp.zeros((2 * RANK, 2 * RANK), F32)
    for i in range(STEPS // 4, (ROWS - STEPS) // 4):
        gram = gram + gram_of(i)
    for side, row0 in enumerate((0, STEPS + ROWS)):
        @pl.when(inside[side])
        def _():
            for level in range(2):
                halos[level, 1 - side].wait_recv()

        @pl.when(jnp.logical_not(inside[side]))
        def _():
            for level in range(2):
                for r in range(STEPS):
                    fields[level, row0 + r] = jnp.zeros((RANK, COLS), F32)

    edge_sweeps(fields, speed, middle, beside, False)

    crossed = remote(
        fields.at[0, pl.ds(STEPS, ROWS)], sketches.at[own], core_send.at[6], core_recv.at[6], {"shot": away}
    )
    crossed.start()
    kept = pltpu.make_async_copy(fields.at[0, pl.ds(STEPS, ROWS)], sketches.at[own], keep_sem.at[0])
    kept.start()

    for i in list(range(STEPS // 4)) + list(range((ROWS - STEPS) // 4, ROWS // 4)):
        gram = gram + gram_of(i)
    gram = gram[:RANK] + gram[RANK:]
    gram = gram[:, :RANK] + gram[:, RANK:]
    packed = jnp.concatenate([gram[:8], gram[8:], jnp.zeros((8, HALF - 2 * RANK), F32)], 1)
    for side, packed in zip((own, away), gram_sum(packed)):
        gram = jnp.concatenate([packed, pltpu.roll(packed, HALF - RANK, 1)], 0)
        high, low = split(lower_inverse(gram) * scale)
        inverses[side, 0] = high
        inverses[side, 1] = low
    crossed.wait_recv()
    kept.wait()
    for side, out in enumerate((left_out, right_out)):
        high, low = (inverses[side, k][:, RANK : 2 * RANK] for k in range(2))
        lhs = jnp.concatenate([jnp.concatenate([high, high], 1), jnp.concatenate([low, low], 1)], 0)

        def put_block(b, carry):
            for r in range(STEPS):
                both = dot(lhs, stacked(sketches[side, b * STEPS + r]))
                value = both[:RANK] + both[RANK:]
                for h in range(2):
                    out.at[b, h].reshape(RANK * STEPS, HALF)[pl.ds(r, RANK, stride=STEPS), :] = (
                        value[:, h * HALF : (h + 1) * HALF]
                    )
            return carry

        lax.fori_loop(0, blocks, put_block, 0, unroll=blocks)

    crossed.wait_send()
    for side in range(2):
        @pl.when(inside[side])
        def _():
            for copy in edges[1 - side]:
                copy.wait_send()
            for level in range(2):
                halos[level, side].wait_send()

    for copy in crossing.values():
        copy.wait_send()
    for copies in handed.values():
        for copy in copies:
            copy.wait_send()


def shards(source_now, source_prev, adjoint_now, adjoint_prev, courant, probe_left, probe_right):
    waves = [a.reshape(WAVES, ROWS, COLS) for a in (source_now, source_prev, adjoint_now, adjoint_prev)]
    any_spec = pl.BlockSpec(memory_space=pl.ANY)
    vmem_spec = pl.BlockSpec(memory_space=pltpu.VMEM)
    dma = pltpu.SemaphoreType.DMA
    count = ROWS // STEPS
    scale = math.sqrt(ROWS * lax.axis_size("strip") * COLS)
    factors = pl.pallas_call(
        functools.partial(main_kernel, scale),
        out_shape=(pltpu.VMEM((count, 2, RANK, STEPS, HALF), F32),) * 2,
        in_specs=[any_spec] * 7,
        out_specs=(vmem_spec, vmem_spec),
        scratch_shapes=[
            pltpu.VMEM((4, count, 2, WAVES, STEPS, HALF), F32),
            pltpu.VMEM((4, ROWS, 2 * WAVES, COLS), BF16),
            pltpu.VMEM((count, 2, RANK, STEPS, HALF), F32),
            pltpu.VMEM((2, 2, RANK, STEPS, HALF), F32),
            pltpu.VMEM((ROWS, COLS), F32),
            pltpu.VMEM((2, STEPS, COLS), F32),
            pltpu.VMEM((TALL, 8, COLS), F32),
            pltpu.VMEM((TALL, 8, COLS), F32),
            pltpu.VMEM((COLS, COLS), BF16),
            pltpu.VMEM((2, TALL, RANK, COLS), F32),
            pltpu.VMEM((2, ROWS, RANK, COLS), F32),
            pltpu.VMEM((2, 2 * RANK, HALF), BF16),
            pltpu.VMEM((RANK, HALF), F32),
            pltpu.VMEM((PLANE - 1, RANK, HALF), F32),
            pltpu.VMEM((RANK, HALF), F32),
            pltpu.VMEM((SIDE - 1, RANK, HALF), F32),
            pltpu.VMEM((8, HALF), F32),
            pltpu.VMEM((2, PLANE, 8, HALF), F32),
            pltpu.VMEM((2, 8, HALF), F32),
            pltpu.VMEM((SIDE - 1, 2, 8, HALF), F32),
            pltpu.VMEM((2, ROWS, RANK, COLS), F32),
            pltpu.VMEM((2, 2, RANK, HALF), BF16),
            pltpu.VMEM((2, TALL, RANK, COLS), F32),
            pltpu.VMEM((2, 2, STEPS, RANK, COLS), F32),
            pltpu.VMEM((2, ROWS, RANK, COLS), F32),
            pltpu.VMEM((2, ROWS, RANK, COLS), F32),
            dma((1 + 2 * count + 8 * count,)),
            dma((2, 3)),
            dma((2, 3)),
            dma((3 * PLANE + 2 * SIDE - 3,)),
            dma((3 * PLANE + 2 * SIDE - 3,)),
            dma((8,)),
            dma((8,)),
            dma((2, 2)),
            dma((2, 2)),
            dma((3, 2)),
            dma((3, 2)),
            dma((1,)),
        ],
        compiler_params=pltpu.CompilerParams(
            collective_id=0, has_side_effects=True, vmem_limit_bytes=56 * 1024 * 1024
        ),
        name="sketch",
    )(*waves, courant, probe_left, probe_right)
    return tuple(factor.transpose(2, 0, 3, 1, 4).reshape(RANK, ROWS, COLS) for factor in factors)


def solution(mesh):
    return jax.shard_map(
        shards,
        mesh=mesh,
        in_specs=(P("shot", None, "strip", None),) * 4 + (P("strip", None),) + (P(None, "strip", None),) * 2,
        out_specs=(P(None, "strip", None), P(None, "strip", None)),
        check_vma=False,
    )
```
